128 devices in a mesh: img: 8 (over z, core), cap: 16 (over y, x).
Axes of the slice: x: 4, y: 4, z: 4, core: 2. Of those that a mesh axis runs over, the one named last changes fastest.
Arguments:
- images: bfloat16 [65536, 256], P('img'), may hold values from -24 to 24
- captions: bfloat16 [8192, 256], P('cap'), may hold values from -4 to 4
- image_logw: float32 [65536], P('img'), may hold values from -1 to 1
- caption_logw: float32 [8192], P('cap'), may hold values from -1 to 1
- image_cot: float32 [65536], P('img'), may hold values from -6 to 6
- caption_cot: float32 [8192], P('cap'), may hold values from -6 to 6
Outputs:
- image_grad: float32 [65536, 256], P(('img', 'cap'))
- caption_grad: float32 [8192, 256], P(('cap', 'img'))
The draws below stay inside these ranges and needn't reach their ends.
All inputs are finite; a program needn't handle non-finite values.
Results may differ from the reference program's by a relative error of at most 0.0029.
Values may be sent and summed in bfloat16 or wider, within the bound.
A program may use at most 128 MiB of HBM per device.

```python
import math
import jax
import jax.numpy as jnp
from jax import lax

E = 256
ITERS = 3
NI = 65536
NC = 8192
N_IMG = 8


def joint_embeddings(key):
    base = jax.random.fold_in(key, 7)
    key_cap, key_img = jax.random.split(base, 2)
    caption_rows = jnp.clip(jax.random.normal(key_cap, (NC, E), jnp.float32), -4.0, 4.0)
    image_rows = jnp.clip(jax.random.normal(key_img, (NI, E), jnp.float32), -4.0, 4.0)
    return (image_rows, caption_rows)


def draw_images(key, part):
    return joint_embeddings(key)[0].astype(jnp.bfloat16)


def draw_captions(key, part):
    return joint_embeddings(key)[1].astype(jnp.bfloat16)


def block_scale(key, shape, cuts, smallest, high):
    def one(axis_at, blocks):
        steps = jax.random.uniform(jax.random.fold_in(jax.random.fold_in(key, 6), axis_at), (blocks,), jnp.float32, smallest / len(cuts), high / len(cuts))
        return jnp.repeat(jnp.exp(steps), shape[axis_at] // blocks).reshape((-1,) + (1,) * (len(shape) - axis_at - 1))

    loudness = one(*cuts[0])
    for cut in cuts[1:]:
        loudness = loudness * one(*cut)
    return loudness


def bell_draw(own_key, extent, deviation, reach, pieces=(), dtype=jnp.bfloat16):
    level = block_scale(own_key, extent, pieces, -0.22, 0.18) if pieces else 1.0
    drawn = jax.random.normal(own_key, extent, jnp.float32) * deviation * level
    return jnp.minimum(jnp.maximum(drawn, -reach), reach).astype(dtype)


def setup_inputs(seed: int = 0) -> dict:
    keys = jax.random.split(jax.random.key(seed), 7)
    images = draw_images(jax.random.fold_in(keys[6], 71), 0)
    captions = draw_captions(jax.random.fold_in(keys[6], 71), 0)
    image_logw = jnp.clip(jax.random.uniform(keys[2], (NI,), jnp.float32, -1.0, 1.0) * block_scale(keys[2], (NI,), ((0, 8),), -0.4, 0.0), -1.0, 1.0)
    caption_logw = jnp.clip(jax.random.uniform(keys[3], (NC,), jnp.float32, -1.0, 1.0) * block_scale(keys[3], (NC,), ((0, 16),), -0.4, 0.0), -1.0, 1.0)
    image_cot = bell_draw(keys[4], (NI,), 1.0, 6.0, ((0, 8),), jnp.float32)
    caption_cot = bell_draw(keys[5], (NC,), 1.0, 6.0, ((0, 16),), jnp.float32)
    return {"images": images, "captions": captions, "image_logw": image_logw, "caption_logw": caption_logw, "image_cot": image_cot, "caption_cot": caption_cot}


SMOOTHING = 0.25

def reference(images, captions, image_logw, caption_logw, image_cot, caption_cot):
    inv_root = 1.0 / math.sqrt(E)
    blocks = N_IMG
    rows = NI // blocks
    x_blocks = images.reshape(blocks, rows, E)

    def tile(block):
        return jnp.dot(block, captions.T, preferred_element_type=jnp.float32) * inv_root

    def row_lse(col_pot):

        def one(block):
            logits = (col_pot[None, :] + tile(block)) / SMOOTHING
            return jax.scipy.special.logsumexp(logits, axis=1)
        return lax.map(one, x_blocks).reshape(NI)

    def col_lse(row_pot):

        def stepper(carry, item):
            logits = (item[1][:, None] + tile(item[0])) / SMOOTHING
            top = jnp.maximum(carry[0], lax.optimization_barrier(jnp.max(logits, axis=0)))
            total = carry[1] * jnp.exp(carry[0] - top) + lax.optimization_barrier(jnp.sum(jnp.exp(logits - top[None, :]), axis=0))
            return ((top, total), None)
        start = (jnp.full((NC,), -jnp.inf, jnp.float32), jnp.zeros((NC,), jnp.float32))
        carry, unused = lax.scan(stepper, start, (x_blocks, row_pot.reshape(blocks, rows)))
        return carry[0] + jnp.log(carry[1])
    col_hist = [jnp.zeros((NC,), jnp.float32)]
    row_hist = []
    for level in range(ITERS):
        row_pot = SMOOTHING * image_logw - SMOOTHING * row_lse(col_hist[-1])
        row_hist.append(row_pot)
        col_hist.append(SMOOTHING * caption_logw - SMOOTHING * col_lse(row_pot))

    def q_rowsum(row_pot, col_pot, col_bar):
        shift = caption_logw - col_pot / SMOOTHING

        def one(item):
            plan = jnp.exp((item[1][:, None] + tile(item[0])) / SMOOTHING - shift[None, :])
            return lax.optimization_barrier(jnp.sum(plan * col_bar[None, :], axis=1))
        return lax.map(one, (x_blocks, row_pot.reshape(blocks, rows))).reshape(NI)

    def r_colsum(row_pot, prev_col, row_bar):

        def stepper(acc, item):
            shift = item[2] - item[1] / SMOOTHING
            plan = jnp.exp((prev_col[None, :] + tile(item[0])) / SMOOTHING - shift[:, None])
            return (acc + lax.optimization_barrier(jnp.sum(plan * item[3][:, None], axis=0)), None)
        acc, unused = lax.scan(stepper, jnp.zeros((NC,), jnp.float32), (x_blocks, row_pot.reshape(blocks, rows), image_logw.reshape(blocks, rows), row_bar.reshape(blocks, rows)))
        return acc
    row_bars = [None] * ITERS
    col_bars = [None] * ITERS
    col_bar = caption_cot
    for level in reversed(range(ITERS)):
        col_bars[level] = col_bar
        row_bar = -q_rowsum(row_hist[level], col_hist[level + 1], col_bar)
        if level == ITERS - 1:
            row_bar = image_cot + row_bar
        row_bars[level] = row_bar
        if level > 0:
            col_bar = -r_colsum(row_hist[level], col_hist[level], row_bar)
    row_stack = jnp.stack(row_hist).reshape(ITERS, blocks, rows).transpose(1, 0, 2)
    rbar_stack = jnp.stack(row_bars).reshape(ITERS, blocks, rows).transpose(1, 0, 2)
    col_stack = jnp.stack(col_hist)
    cbar_stack = jnp.stack(col_bars)

    def final(acc, item):
        block, rpots, rbars, logw = item
        scores = tile(block)
        adjoint = jnp.zeros((rows, NC), jnp.float32)
        for level in reversed(range(ITERS)):
            shift_col = caption_logw - col_stack[level + 1] / SMOOTHING
            col_plan = jnp.exp((rpots[level][:, None] + scores) / SMOOTHING - shift_col[None, :])
            adjoint = adjoint - col_plan * cbar_stack[level][None, :]
            shift_row = logw - rpots[level] / SMOOTHING
            row_plan = jnp.exp((col_stack[level][None, :] + scores) / SMOOTHING - shift_row[:, None])
            adjoint = adjoint - row_plan * rbars[level][:, None]
        rounded = adjoint.astype(jnp.bfloat16)
        grad_rows = jnp.dot(rounded, captions, preferred_element_type=jnp.float32) * inv_root
        acc = acc + jnp.dot(rounded.T, block, preferred_element_type=jnp.float32) * inv_root
        return (acc, grad_rows)
    caption_grad, image_rows = lax.scan(final, jnp.zeros((NC, E), jnp.float32), (x_blocks, row_stack, rbar_stack, image_logw.reshape(blocks, rows)))
    return (image_rows.reshape(NI, E), caption_grad)
```

```python
import math

import jax
import jax.numpy as jnp
from jax import lax
from jax.sharding import PartitionSpec as P

ITERS = 3


SMOOTHING = 0.25


def gathered_lse(part, axis):
    pieces = lax.all_gather(part, axis)
    top = jnp.max(pieces, axis=0)
    return top + jnp.log(jnp.sum(jnp.exp(pieces - top[None]), axis=0))


def gathered_sum(part, axis):
    return jnp.sum(lax.all_gather(part, axis), axis=0)


def body(images, captions, image_logw, caption_logw, image_cot, caption_cot):
    inv_root = 1.0 / math.sqrt(images.shape[1])

    def get_tile():
        return jnp.dot(images, captions.T, preferred_element_type=jnp.float32) * inv_root

    col_hist = [jnp.zeros((captions.shape[0],), jnp.float32)]
    row_hist = []
    for level in range(ITERS):
        scores = get_tile()
        logits = (col_hist[-1][None, :] + scores) / SMOOTHING
        top = jnp.max(logits, axis=1)
        part = top + jnp.log(jnp.sum(jnp.exp(logits - top[:, None]), axis=1))
        row_pot = SMOOTHING * image_logw - SMOOTHING * gathered_lse(part, "cap")
        row_hist.append(row_pot)
        logits = (row_pot[:, None] + scores) / SMOOTHING
        top = jnp.max(logits, axis=0)
        part = top + jnp.log(jnp.sum(jnp.exp(logits - top[None, :]), axis=0))
        col_hist.append(SMOOTHING * caption_logw - SMOOTHING * gathered_lse(part, "img"))
    adjoint = jnp.zeros((images.shape[0], captions.shape[0]), jnp.float32)
    col_bar = caption_cot
    for level in reversed(range(ITERS)):
        scores = get_tile()
        row_pot = row_hist[level]
        shift_col = caption_logw - col_hist[level + 1] / SMOOTHING
        col_plan = jnp.exp((row_pot[:, None] + scores) / SMOOTHING - shift_col[None, :])
        weighted = col_plan * col_bar[None, :]
        adjoint = adjoint - weighted
        row_bar = -gathered_sum(jnp.sum(weighted, axis=1), "cap")
        if level == ITERS - 1:
            row_bar = image_cot + row_bar
        shift_row = image_logw - row_pot / SMOOTHING
        row_plan = jnp.exp((col_hist[level][None, :] + scores) / SMOOTHING - shift_row[:, None])
        weighted = row_plan * row_bar[:, None]
        adjoint = adjoint - weighted
        if level > 0:
            col_bar = -gathered_sum(jnp.sum(weighted, axis=0), "img")
    rounded = adjoint.astype(jnp.bfloat16)
    image_grad = lax.psum_scatter(
        jnp.dot(rounded, captions, preferred_element_type=jnp.float32) * inv_root,
        "cap",
        scatter_dimension=0,
        tiled=True,
    )
    caption_grad = lax.psum_scatter(
        lax.dot_general(
            rounded, images, (((0,), (0,)), ((), ())), preferred_element_type=jnp.float32
        )
        * inv_root,
        "img",
        scatter_dimension=0,
        tiled=True,
    )
    return (image_grad, caption_grad)


def solution(mesh):
    in_specs = (P("img", None), P("cap", None), P("img"), P("cap"), P("img"), P("cap"))
    out_specs = (P(("img", "cap"), None), P(("cap", "img"), None))
    return jax.shard_map(body, mesh=mesh, in_specs=in_specs, out_specs=out_specs, check_vma=False)
```

```python
import functools
import math

import jax
import jax.numpy as jnp
from jax import lax
from jax.experimental import pallas as pl
from jax.experimental.pallas import tpu as pltpu

MESH = pl.DeviceIdType.MESH


def _peer(axis, k, n):
    me_img = lax.axis_index("img")
    me_cap = lax.axis_index("cap")
    if axis == "cap":
        return (me_img, lax.rem(me_cap + k, n))
    return (lax.rem(me_img + k, n), me_cap)


def _combine_kernel(axis, n, mode, x_ref, o_ref, buf, send_sem, recv_sem):
    barrier = pltpu.get_barrier_semaphore()
    for k in range(1, n):
        pl.semaphore_signal(barrier, inc=1, device_id=_peer(axis, k, n), device_id_type=MESH)
    pl.semaphore_wait(barrier, n - 1)
    copies = []
    for k in range(1, n):
        copy = pltpu.make_async_remote_copy(
            src_ref=x_ref,
            dst_ref=buf.at[k],
            send_sem=send_sem.at[k],
            recv_sem=recv_sem.at[k],
            device_id=_peer(axis, k, n),
            device_id_type=MESH,
        )
        copy.start()
        copies.append(copy)
    for copy in copies:
        copy.wait()
    x = x_ref[...]
    if mode == "sum":
        acc = x
        for k in range(1, n):
            acc = acc + buf[k]
    else:
        top = x
        for k in range(1, n):
            top = jnp.maximum(top, buf[k])
        tot = jnp.exp(x - top)
        for k in range(1, n):
            tot = tot + jnp.exp(buf[k] - top)
        acc = top + jnp.log(tot)
    o_ref[...] = acc


def combine(x, axis, n, mode, cid):
    size = x.shape[0]
    rows = size // 128
    x2 = x.reshape(rows, 128)
    out = pl.pallas_call(
        functools.partial(_combine_kernel, axis, n, mode),
        out_shape=jax.ShapeDtypeStruct((rows, 128), jnp.float32),
        in_specs=[pl.BlockSpec(memory_space=pltpu.VMEM)],
        out_specs=pl.BlockSpec(memory_space=pltpu.VMEM),
        scratch_shapes=[
            pltpu.VMEM((n, rows, 128), jnp.float32),
            pltpu.SemaphoreType.DMA((n,)),
            pltpu.SemaphoreType.DMA((n,)),
        ],
        compiler_params=pltpu.CompilerParams(collective_id=cid, has_side_effects=True),
    )(x2)
    return out.reshape(size)

from jax.sharding import PartitionSpec as P

ITERS = 3


SMOOTHING = 0.25


_IDS = {("cap", "lse"): 0, ("img", "lse"): 1, ("cap", "sum"): 2, ("img", "sum"): 3}


def gathered_lse(part, axis):
    return combine(part, axis, lax.axis_size(axis), "lse", _IDS[(axis, "lse")])


def gathered_sum(part, axis):
    return combine(part, axis, lax.axis_size(axis), "sum", _IDS[(axis, "sum")])


def body(images, captions, image_logw, caption_logw, image_cot, caption_cot):
    inv_root = 1.0 / math.sqrt(images.shape[1])

    def get_tile():
        return jnp.dot(images, captions.T, preferred_element_type=jnp.float32) * inv_root

    col_hist = [jnp.zeros((captions.shape[0],), jnp.float32)]
    row_hist = []
    for level in range(ITERS):
        scores = get_tile()
        logits = (col_hist[-1][None, :] + scores) / SMOOTHING
        top = jnp.max(logits, axis=1)
        part = top + jnp.log(jnp.sum(jnp.exp(logits - top[:, None]), axis=1))
        row_pot = SMOOTHING * image_logw - SMOOTHING * gathered_lse(part, "cap")
        row_hist.append(row_pot)
        logits = (row_pot[:, None] + scores) / SMOOTHING
        top = jnp.max(logits, axis=0)
        part = top + jnp.log(jnp.sum(jnp.exp(logits - top[None, :]), axis=0))
        col_hist.append(SMOOTHING * caption_logw - SMOOTHING * gathered_lse(part, "img"))
    adjoint = jnp.zeros((images.shape[0], captions.shape[0]), jnp.float32)
    col_bar = caption_cot
    for level in reversed(range(ITERS)):
        scores = get_tile()
        row_pot = row_hist[level]
        shift_col = caption_logw - col_hist[level + 1] / SMOOTHING
        col_plan = jnp.exp((row_pot[:, None] + scores) / SMOOTHING - shift_col[None, :])
        weighted = col_plan * col_bar[None, :]
        adjoint = adjoint - weighted
        row_bar = -gathered_sum(jnp.sum(weighted, axis=1), "cap")
        if level == ITERS - 1:
            row_bar = image_cot + row_bar
        shift_row = image_logw - row_pot / SMOOTHING
        row_plan = jnp.exp((col_hist[level][None, :] + scores) / SMOOTHING - shift_row[:, None])
        weighted = row_plan * row_bar[:, None]
        adjoint = adjoint - weighted
        if level > 0:
            col_bar = -gathered_sum(jnp.sum(weighted, axis=0), "img")
    rounded = adjoint.astype(jnp.bfloat16)
    image_grad = lax.psum_scatter(
        jnp.dot(rounded, captions, preferred_element_type=jnp.float32) * inv_root,
        "cap",
        scatter_dimension=0,
        tiled=True,
    )
    caption_grad = lax.psum_scatter(
        lax.dot_general(
            rounded, images, (((0,), (0,)), ((), ())), preferred_element_type=jnp.float32
        )
        * inv_root,
        "img",
        scatter_dimension=0,
        tiled=True,
    )
    return (image_grad, caption_grad)


def solution(mesh):
    in_specs = (P("img", None), P("cap", None), P("img"), P("cap"), P("img"), P("cap"))
    out_specs = (P(("img", "cap"), None), P(("cap", "img"), None))
    return jax.shard_map(body, mesh=mesh, in_specs=in_specs, out_specs=out_specs, check_vma=False)
```

```python
import functools
import math

import jax
import jax.numpy as jnp
from jax import lax
from jax.experimental import pallas as pl
from jax.experimental.pallas import tpu as pltpu

MESH = pl.DeviceIdType.MESH


def _peer(axis, k, n):
    me_img = lax.axis_index("img")
    me_cap = lax.axis_index("cap")
    if axis == "cap":
        return (me_img, lax.rem(me_cap + k, n))
    return (lax.rem(me_img + k, n), me_cap)


def _combine_kernel(axis, n, mode, x_ref, o_ref, buf, send_sem, recv_sem):
    barrier = pltpu.get_barrier_semaphore()
    for k in range(1, n):
        pl.semaphore_signal(barrier, inc=1, device_id=_peer(axis, k, n), device_id_type=MESH)
    pl.semaphore_wait(barrier, n - 1)
    copies = []
    for k in range(1, n):
        copy = pltpu.make_async_remote_copy(
            src_ref=x_ref,
            dst_ref=buf.at[k],
            send_sem=send_sem.at[k],
            recv_sem=recv_sem.at[k],
            device_id=_peer(axis, k, n),
            device_id_type=MESH,
        )
        copy.start()
        copies.append(copy)
    for copy in copies:
        copy.wait()
    x = x_ref[...]
    if mode == "sum":
        acc = x
        for k in range(1, n):
            acc = acc + buf[k]
    else:
        top = x
        for k in range(1, n):
            top = jnp.maximum(top, buf[k])
        tot = jnp.exp(x - top)
        for k in range(1, n):
            tot = tot + jnp.exp(buf[k] - top)
        acc = top + jnp.log(tot)
    o_ref[...] = acc


def combine(x, axis, n, mode, cid):
    size = x.shape[0]
    rows = size // 128
    x2 = x.reshape(rows, 128)
    out = pl.pallas_call(
        functools.partial(_combine_kernel, axis, n, mode),
        out_shape=jax.ShapeDtypeStruct((rows, 128), jnp.float32),
        in_specs=[pl.BlockSpec(memory_space=pltpu.VMEM)],
        out_specs=pl.BlockSpec(memory_space=pltpu.VMEM),
        scratch_shapes=[
            pltpu.VMEM((n, rows, 128), jnp.float32),
            pltpu.SemaphoreType.DMA((n,)),
            pltpu.SemaphoreType.DMA((n,)),
        ],
        compiler_params=pltpu.CompilerParams(collective_id=cid, has_side_effects=True),
    )(x2)
    return out.reshape(size)

from jax.sharding import PartitionSpec as P

ITERS = 3


SMOOTHING = 0.25


_IDS = {("cap", "lse"): 0, ("img", "lse"): 1, ("cap", "sum"): 2, ("img", "sum"): 3}


def gathered_lse(part, axis):
    return combine(part, axis, lax.axis_size(axis), "lse", _IDS[(axis, "lse")])


def gathered_sum(part, axis):
    return combine(part, axis, lax.axis_size(axis), "sum", _IDS[(axis, "sum")])


TM = 512


def _scores(img_ref, cap_ref, inv_root):
    return lax.dot_general(
        img_ref[...], cap_ref[...], (((1,), (1,)), ((), ())), preferred_element_type=jnp.float32
    ) * inv_root


def _row_kernel(mode, inv_root, img_ref, cap_ref, a_ref, b_ref, w_ref, o_ref):
    s = _scores(img_ref, cap_ref, inv_root)
    if mode == "lse":
        x = (b_ref[...] + s) / SMOOTHING
        top = jnp.max(x, axis=1, keepdims=True)
        o_ref[...] = top + jnp.log(jnp.sum(jnp.exp(x - top), axis=1, keepdims=True))
    else:
        plan = jnp.exp((a_ref[...] + s) / SMOOTHING - b_ref[...])
        o_ref[...] = jnp.sum(plan * w_ref[...], axis=1, keepdims=True)


def row_pass(mode, images, captions, a, b, w):
    n, e = images.shape
    c = captions.shape[0]
    inv_root = 1.0 / math.sqrt(e)
    out = pl.pallas_call(
        functools.partial(_row_kernel, mode, inv_root),
        out_shape=jax.ShapeDtypeStruct((n, 1), jnp.float32),
        grid=(n // TM,),
        in_specs=[
            pl.BlockSpec((TM, e), lambda i: (i, 0)),
            pl.BlockSpec((c, e), lambda i: (0, 0)),
            pl.BlockSpec((TM, 1), lambda i: (i, 0)),
            pl.BlockSpec((1, c), lambda i: (0, 0)),
            pl.BlockSpec((1, c), lambda i: (0, 0)),
        ],
        out_specs=pl.BlockSpec((TM, 1), lambda i: (i, 0)),
        cost_estimate=pl.CostEstimate(
            flops=2 * n * c * e, transcendentals=n * c, bytes_accessed=n * e * 2 + c * e * 2
        ),
    )(images, captions, a.reshape(n, 1), b.reshape(1, c), w.reshape(1, c))
    return out.reshape(n)


def _col_kernel(mode, inv_root, img_ref, cap_ref, a_ref, b_ref, w_ref, o_ref, top_ref, tot_ref):
    step = pl.program_id(0)
    s = _scores(img_ref, cap_ref, inv_root)
    if mode == "lse":
        x = (a_ref[...] + s) / SMOOTHING

        @pl.when(step == 0)
        def _():
            top_ref[...] = jnp.full(top_ref.shape, -jnp.inf, jnp.float32)
            tot_ref[...] = jnp.zeros(tot_ref.shape, jnp.float32)

        old = top_ref[...]
        top = jnp.maximum(old, jnp.max(x, axis=0, keepdims=True))
        tot_ref[...] = tot_ref[...] * jnp.exp(old - top) + jnp.sum(jnp.exp(x - top), axis=0, keepdims=True)
        top_ref[...] = top

        @pl.when(step == pl.num_programs(0) - 1)
        def _():
            o_ref[...] = top_ref[...] + jnp.log(tot_ref[...])
    else:
        plan = jnp.exp((b_ref[...] + s) / SMOOTHING - a_ref[...])

        @pl.when(step == 0)
        def _():
            tot_ref[...] = jnp.zeros(tot_ref.shape, jnp.float32)

        tot_ref[...] += jnp.sum(plan * w_ref[...], axis=0, keepdims=True)

        @pl.when(step == pl.num_programs(0) - 1)
        def _():
            o_ref[...] = tot_ref[...]


def col_pass(mode, images, captions, a, w, b):
    n, e = images.shape
    c = captions.shape[0]
    inv_root = 1.0 / math.sqrt(e)
    out = pl.pallas_call(
        functools.partial(_col_kernel, mode, inv_root),
        out_shape=jax.ShapeDtypeStruct((1, c), jnp.float32),
        grid=(n // TM,),
        in_specs=[
            pl.BlockSpec((TM, e), lambda i: (i, 0)),
            pl.BlockSpec((c, e), lambda i: (0, 0)),
            pl.BlockSpec((TM, 1), lambda i: (i, 0)),
            pl.BlockSpec((1, c), lambda i: (0, 0)),
            pl.BlockSpec((TM, 1), lambda i: (i, 0)),
        ],
        out_specs=pl.BlockSpec((1, c), lambda i: (0, 0)),
        scratch_shapes=[pltpu.VMEM((1, c), jnp.float32), pltpu.VMEM((1, c), jnp.float32)],
        cost_estimate=pl.CostEstimate(
            flops=2 * n * c * e, transcendentals=n * c, bytes_accessed=n * e * 2 + c * e * 2
        ),
    )(images, captions, a.reshape(n, 1), b.reshape(1, c), w.reshape(n, 1))
    return out.reshape(c)


def _final_kernel(inv_root, img_ref, cap_ref, rows_ref, cols_ref, ig_ref, cg_ref):
    step = pl.program_id(0)
    s = _scores(img_ref, cap_ref, inv_root)
    rows = rows_ref[...]
    cols = cols_ref[...]
    logw_r = rows[:, 6:7]
    logw_c = cols[7:8, :]
    adjoint = jnp.zeros(s.shape, jnp.float32)
    for level in reversed(range(ITERS)):
        f = rows[:, level:level + 1]
        fb = rows[:, 3 + level:4 + level]
        g_prev = cols[level:level + 1, :]
        g = cols[level + 1:level + 2, :]
        gb = cols[4 + level:5 + level, :]
        col_plan = jnp.exp((f + s) / SMOOTHING - (logw_c - g / SMOOTHING))
        adjoint = adjoint - col_plan * gb
        row_plan = jnp.exp((g_prev + s) / SMOOTHING - (logw_r - f / SMOOTHING))
        adjoint = adjoint - row_plan * fb
    rounded = adjoint.astype(jnp.bfloat16)
    ig_ref[...] = jnp.dot(rounded, cap_ref[...], preferred_element_type=jnp.float32) * inv_root

    @pl.when(step == 0)
    def _():
        cg_ref[...] = jnp.zeros(cg_ref.shape, jnp.float32)

    cg_ref[...] += lax.dot_general(
        rounded, img_ref[...], (((0,), (0,)), ((), ())), preferred_element_type=jnp.float32
    ) * inv_root


def final_pass(images, captions, rows, cols):
    n, e = images.shape
    c = captions.shape[0]
    inv_root = 1.0 / math.sqrt(e)
    return pl.pallas_call(
        functools.partial(_final_kernel, inv_root),
        out_shape=(
            jax.ShapeDtypeStruct((n, e), jnp.float32),
            jax.ShapeDtypeStruct((c, e), jnp.float32),
        ),
        grid=(n // TM,),
        in_specs=[
            pl.BlockSpec((TM, e), lambda i: (i, 0)),
            pl.BlockSpec((c, e), lambda i: (0, 0)),
            pl.BlockSpec((TM, 8), lambda i: (i, 0)),
            pl.BlockSpec((8, c), lambda i: (0, 0)),
        ],
        out_specs=(
            pl.BlockSpec((TM, e), lambda i: (i, 0)),
            pl.BlockSpec((c, e), lambda i: (0, 0)),
        ),
        cost_estimate=pl.CostEstimate(
            flops=6 * n * c * e, transcendentals=6 * n * c, bytes_accessed=n * e * 6 + c * e * 6
        ),
    )(images, captions, rows, cols)


def body(images, captions, image_logw, caption_logw, image_cot, caption_cot):
    n = images.shape[0]
    c = captions.shape[0]
    zeros_r = jnp.zeros((n,), jnp.float32)
    zeros_c = jnp.zeros((c,), jnp.float32)
    col_hist = [zeros_c]
    row_hist = []
    for level in range(ITERS):
        part = row_pass("lse", images, captions, zeros_r, col_hist[-1], zeros_c)
        row_pot = SMOOTHING * image_logw - SMOOTHING * gathered_lse(part, "cap")
        row_hist.append(row_pot)
        part = col_pass("lse", images, captions, row_pot, zeros_r, zeros_c)
        col_hist.append(SMOOTHING * caption_logw - SMOOTHING * gathered_lse(part, "img"))
    col_bar = caption_cot
    row_bars = [None] * ITERS
    col_bars = [None] * ITERS
    for level in reversed(range(ITERS)):
        col_bars[level] = col_bar
        shift_col = caption_logw - col_hist[level + 1] / SMOOTHING
        part = row_pass("wsum", images, captions, row_hist[level], shift_col, col_bar)
        row_bar = -gathered_sum(part, "cap")
        if level == ITERS - 1:
            row_bar = image_cot + row_bar
        row_bars[level] = row_bar
        if level > 0:
            shift_row = image_logw - row_hist[level] / SMOOTHING
            part = col_pass("wsum", images, captions, shift_row, row_bar, col_hist[level])
            col_bar = -gathered_sum(part, "img")
    rows = jnp.stack(row_hist + row_bars + [image_logw, zeros_r], axis=1)
    cols = jnp.stack(col_hist + col_bars + [caption_logw], axis=0)
    ig_part, cg_part = final_pass(images, captions, rows, cols)
    image_grad = lax.psum_scatter(ig_part, "cap", scatter_dimension=0, tiled=True)
    caption_grad = lax.psum_scatter(cg_part, "img", scatter_dimension=0, tiled=True)
    return (image_grad, caption_grad)


def solution(mesh):
    in_specs = (P("img", None), P("cap", None), P("img"), P("cap"), P("img"), P("cap"))
    out_specs = (P(("img", "cap"), None), P(("cap", "img"), None))
    return jax.shard_map(body, mesh=mesh, in_specs=in_specs, out_specs=out_specs, check_vma=False)
```

```python
import functools
import math

import jax
import jax.numpy as jnp
from jax import lax
from jax.experimental import pallas as pl
from jax.experimental.pallas import tpu as pltpu

MESH = pl.DeviceIdType.MESH


def _peer(axis, k, n):
    me_img = lax.axis_index("img")
    me_cap = lax.axis_index("cap")
    if axis == "cap":
        return (me_img, lax.rem(me_cap + k, n))
    return (lax.rem(me_img + k, n), me_cap)


def _combine_kernel(axis, n, mode, x_ref, o_ref, buf, send_sem, recv_sem):
    barrier = pltpu.get_barrier_semaphore()
    for k in range(1, n):
        pl.semaphore_signal(barrier, inc=1, device_id=_peer(axis, k, n), device_id_type=MESH)
    pl.semaphore_wait(barrier, n - 1)
    copies = []
    for k in range(1, n):
        copy = pltpu.make_async_remote_copy(
            src_ref=x_ref,
            dst_ref=buf.at[k],
            send_sem=send_sem.at[k],
            recv_sem=recv_sem.at[k],
            device_id=_peer(axis, k, n),
            device_id_type=MESH,
        )
        copy.start()
        copies.append(copy)
    for copy in copies:
        copy.wait()
    x = x_ref[...]
    if mode == "sum":
        acc = x
        for k in range(1, n):
            acc = acc + buf[k]
    else:
        top = x
        for k in range(1, n):
            top = jnp.maximum(top, buf[k])
        tot = jnp.exp(x - top)
        for k in range(1, n):
            tot = tot + jnp.exp(buf[k] - top)
        acc = top + jnp.log(tot)
    o_ref[...] = acc


def combine(x, axis, n, mode, cid):
    size = x.shape[0]
    rows = size // 128
    x2 = x.reshape(rows, 128)
    out = pl.pallas_call(
        functools.partial(_combine_kernel, axis, n, mode),
        out_shape=jax.ShapeDtypeStruct((rows, 128), jnp.float32),
        in_specs=[pl.BlockSpec(memory_space=pltpu.VMEM)],
        out_specs=pl.BlockSpec(memory_space=pltpu.VMEM),
        scratch_shapes=[
            pltpu.VMEM((n, rows, 128), jnp.float32),
            pltpu.SemaphoreType.DMA((n,)),
            pltpu.SemaphoreType.DMA((n,)),
        ],
        compiler_params=pltpu.CompilerParams(collective_id=cid, has_side_effects=True),
    )(x2)
    return out.reshape(size)

from jax.sharding import PartitionSpec as P

ITERS = 3


SMOOTHING = 0.25


_IDS = {("cap", "lse"): 0, ("img", "lse"): 1, ("cap", "sum"): 2, ("img", "sum"): 3}


def gathered_lse(part, axis):
    return combine(part, axis, lax.axis_size(axis), "lse", _IDS[(axis, "lse")])


def gathered_sum(part, axis):
    return combine(part, axis, lax.axis_size(axis), "sum", _IDS[(axis, "sum")])


TM = 1024
INV_EPS = 1.0 / SMOOTHING


def _scores_t(img_ref, cap_ref, inv_root):
    return lax.dot_general(
        cap_ref[...], img_ref[...], (((1,), (1,)), ((), ())), preferred_element_type=jnp.float32
    ) * inv_root


def _lane_chunks(x):
    return [x[:, k * 128:(k + 1) * 128] for k in range(x.shape[1] // 128)]


def _row_kernel(mode, inv_root, img_ref, cap_ref, a_ref, b_ref, w_ref, o_ref):
    s = _scores_t(img_ref, cap_ref, inv_root)
    if mode == "lse":
        x = (b_ref[...] + s) * INV_EPS
        top = jnp.max(x, axis=0, keepdims=True)
        o_ref[...] = top + jnp.log(jnp.sum(jnp.exp(x - top), axis=0, keepdims=True))
    else:
        plan = jnp.exp((a_ref[...] + s) * INV_EPS - b_ref[...])
        o_ref[...] = jnp.sum(plan * w_ref[...], axis=0, keepdims=True)


def _specs(n, c, e):
    return [
        pl.BlockSpec((TM, e), lambda i: (i, 0)),
        pl.BlockSpec((c, e), lambda i: (0, 0)),
        pl.BlockSpec((1, TM), lambda i: (0, i)),
        pl.BlockSpec((c, 1), lambda i: (0, 0)),
    ]


def row_pass(mode, images, captions, a, b, w):
    n, e = images.shape
    c = captions.shape[0]
    inv_root = 1.0 / math.sqrt(e)
    out = pl.pallas_call(
        functools.partial(_row_kernel, mode, inv_root),
        out_shape=jax.ShapeDtypeStruct((1, n), jnp.float32),
        grid=(n // TM,),
        in_specs=_specs(n, c, e) + [pl.BlockSpec((c, 1), lambda i: (0, 0))],
        out_specs=pl.BlockSpec((1, TM), lambda i: (0, i)),
        cost_estimate=pl.CostEstimate(
            flops=2 * n * c * e, transcendentals=n * c, bytes_accessed=n * e * 2 + c * e * 2
        ),
    )(images, captions, a.reshape(1, n), b.reshape(c, 1), w.reshape(c, 1))
    return out.reshape(n)


def _col_kernel(mode, inv_root, img_ref, cap_ref, a_ref, b_ref, w_ref, o_ref, top_ref, tot_ref):
    step = pl.program_id(0)
    s = _scores_t(img_ref, cap_ref, inv_root)
    if mode == "lse":
        chunks = _lane_chunks((a_ref[...] + s) * INV_EPS)

        @pl.when(step == 0)
        def _():
            top_ref[...] = jnp.full(top_ref.shape, -jnp.inf, jnp.float32)
            tot_ref[...] = jnp.zeros(tot_ref.shape, jnp.float32)

        cmax = chunks[0]
        for piece in chunks[1:]:
            cmax = jnp.maximum(cmax, piece)
        old = top_ref[...]
        top = jnp.maximum(old, cmax)
        tot = tot_ref[...] * jnp.exp(old - top)
        for piece in chunks:
            tot = tot + jnp.exp(piece - top)
        tot_ref[...] = tot
        top_ref[...] = top

        @pl.when(step == pl.num_programs(0) - 1)
        def _():
            t = top_ref[...]
            m = jnp.max(t, axis=1, keepdims=True)
            o_ref[...] = m + jnp.log(jnp.sum(tot_ref[...] * jnp.exp(t - m), axis=1, keepdims=True))
    else:
        plan = jnp.exp((b_ref[...] + s) * INV_EPS - a_ref[...])
        chunks = _lane_chunks(plan * w_ref[...])

        @pl.when(step == 0)
        def _():
            tot_ref[...] = jnp.zeros(tot_ref.shape, jnp.float32)

        acc = chunks[0]
        for piece in chunks[1:]:
            acc = acc + piece
        tot_ref[...] += acc

        @pl.when(step == pl.num_programs(0) - 1)
        def _():
            o_ref[...] = jnp.sum(tot_ref[...], axis=1, keepdims=True)


def col_pass(mode, images, captions, a, w, b):
    n, e = images.shape
    c = captions.shape[0]
    inv_root = 1.0 / math.sqrt(e)
    out = pl.pallas_call(
        functools.partial(_col_kernel, mode, inv_root),
        out_shape=jax.ShapeDtypeStruct((c, 1), jnp.float32),
        grid=(n // TM,),
        in_specs=_specs(n, c, e) + [pl.BlockSpec((1, TM), lambda i: (0, i))],
        out_specs=pl.BlockSpec((c, 1), lambda i: (0, 0)),
        scratch_shapes=[pltpu.VMEM((c, 128), jnp.float32), pltpu.VMEM((c, 128), jnp.float32)],
        cost_estimate=pl.CostEstimate(
            flops=2 * n * c * e, transcendentals=n * c, bytes_accessed=n * e * 2 + c * e * 2
        ),
    )(images, captions, a.reshape(1, n), b.reshape(c, 1), w.reshape(1, n))
    return out.reshape(c)


def _final_kernel(inv_root, img_ref, cap_ref, rows_ref, cols_ref, ig_ref, cg_ref):
    step = pl.program_id(0)
    s = _scores_t(img_ref, cap_ref, inv_root)
    rows = rows_ref[...]
    cols = cols_ref[...]
    logw_r = rows[6:7, :]
    logw_c = cols[:, 7:8]
    adjoint = jnp.zeros(s.shape, jnp.float32)
    for level in reversed(range(ITERS)):
        f = rows[level:level + 1, :]
        fb = rows[3 + level:4 + level, :]
        g_prev = cols[:, level:level + 1]
        g = cols[:, level + 1:level + 2]
        gb = cols[:, 4 + level:5 + level]
        col_plan = jnp.exp((f + s) * INV_EPS - (logw_c - g * INV_EPS))
        adjoint = adjoint - col_plan * gb
        row_plan = jnp.exp((g_prev + s) * INV_EPS - (logw_r - f * INV_EPS))
        adjoint = adjoint - row_plan * fb
    rounded = adjoint.astype(jnp.bfloat16)
    ig_ref[...] = lax.dot_general(
        rounded, cap_ref[...], (((0,), (0,)), ((), ())), preferred_element_type=jnp.float32
    ) * inv_root

    @pl.when(step == 0)
    def _():
        cg_ref[...] = jnp.zeros(cg_ref.shape, jnp.float32)

    cg_ref[...] += jnp.dot(rounded, img_ref[...], preferred_element_type=jnp.float32) * inv_root


def final_pass(images, captions, rows, cols):
    n, e = images.shape
    c = captions.shape[0]
    inv_root = 1.0 / math.sqrt(e)
    return pl.pallas_call(
        functools.partial(_final_kernel, inv_root),
        out_shape=(
            jax.ShapeDtypeStruct((n, e), jnp.float32),
            jax.ShapeDtypeStruct((c, e), jnp.float32),
        ),
        grid=(n // TM,),
        in_specs=[
            pl.BlockSpec((TM, e), lambda i: (i, 0)),
            pl.BlockSpec((c, e), lambda i: (0, 0)),
            pl.BlockSpec((8, TM), lambda i: (0, i)),
            pl.BlockSpec((c, 8), lambda i: (0, 0)),
        ],
        out_specs=(
            pl.BlockSpec((TM, e), lambda i: (i, 0)),
            pl.BlockSpec((c, e), lambda i: (0, 0)),
        ),
        cost_estimate=pl.CostEstimate(
            flops=6 * n * c * e, transcendentals=6 * n * c, bytes_accessed=n * e * 6 + c * e * 6
        ),
    )(images, captions, rows, cols)


def body(images, captions, image_logw, caption_logw, image_cot, caption_cot):
    n = images.shape[0]
    c = captions.shape[0]
    zeros_r = jnp.zeros((n,), jnp.float32)
    zeros_c = jnp.zeros((c,), jnp.float32)
    col_hist = [zeros_c]
    row_hist = []
    for level in range(ITERS):
        part = row_pass("lse", images, captions, zeros_r, col_hist[-1], zeros_c)
        row_pot = SMOOTHING * image_logw - SMOOTHING * gathered_lse(part, "cap")
        row_hist.append(row_pot)
        part = col_pass("lse", images, captions, row_pot, zeros_r, zeros_c)
        col_hist.append(SMOOTHING * caption_logw - SMOOTHING * gathered_lse(part, "img"))
    col_bar = caption_cot
    row_bars = [None] * ITERS
    col_bars = [None] * ITERS
    for level in reversed(range(ITERS)):
        col_bars[level] = col_bar
        shift_col = caption_logw - col_hist[level + 1] / SMOOTHING
        part = row_pass("wsum", images, captions, row_hist[level], shift_col, col_bar)
        row_bar = -gathered_sum(part, "cap")
        if level == ITERS - 1:
            row_bar = image_cot + row_bar
        row_bars[level] = row_bar
        if level > 0:
            shift_row = image_logw - row_hist[level] / SMOOTHING
            part = col_pass("wsum", images, captions, shift_row, row_bar, col_hist[level])
            col_bar = -gathered_sum(part, "img")
    rows = jnp.stack(row_hist + row_bars + [image_logw, zeros_r], axis=0)
    cols = jnp.stack(col_hist + col_bars + [caption_logw], axis=1)
    ig_part, cg_part = final_pass(images, captions, rows, cols)
    image_grad = lax.psum_scatter(ig_part, "cap", scatter_dimension=0, tiled=True)
    caption_grad = lax.psum_scatter(cg_part, "img", scatter_dimension=0, tiled=True)
    return (image_grad, caption_grad)


def solution(mesh):
    in_specs = (P("img", None), P("cap", None), P("img"), P("cap"), P("img"), P("cap"))
    out_specs = (P(("img", "cap"), None), P(("cap", "img"), None))
    return jax.shard_map(body, mesh=mesh, in_specs=in_specs, out_specs=out_specs, check_vma=False)
```

```python
import functools
import math

import jax
import jax.numpy as jnp
from jax import lax
from jax.experimental import pallas as pl
from jax.experimental.pallas import tpu as pltpu

MESH = pl.DeviceIdType.MESH
AXES = ("img", "cy", "cx")


def _peer(group, k):
    idx = {name: lax.axis_index(name) for name in AXES}
    total = 1
    lin = 0
    for name, size in group:
        lin = lin * size + idx[name]
        total *= size
    lin = lax.rem(lin + k, total)
    for name, size in reversed(group):
        idx[name] = lax.rem(lin, size)
        lin = lin // size
    return tuple(idx[name] for name in AXES)


def _combine_kernel(group, n, mode, x_ref, o_ref, buf, send_sem, recv_sem):
    barrier = pltpu.get_barrier_semaphore()
    for k in range(1, n):
        pl.semaphore_signal(barrier, inc=1, device_id=_peer(group, k), device_id_type=MESH)
    pl.semaphore_wait(barrier, n - 1)
    copies = []
    for k in range(1, n):
        copy = pltpu.make_async_remote_copy(
            src_ref=x_ref,
            dst_ref=buf.at[k],
            send_sem=send_sem.at[k],
            recv_sem=recv_sem.at[k],
            device_id=_peer(group, k),
            device_id_type=MESH,
        )
        copy.start()
        copies.append(copy)
    for copy in copies:
        copy.wait()
    x = x_ref[...]
    if mode == "sum":
        acc = x
        for k in range(1, n):
            acc = acc + buf[k]
    else:
        top = x
        for k in range(1, n):
            top = jnp.maximum(top, buf[k])
        tot = jnp.exp(x - top)
        for k in range(1, n):
            tot = tot + jnp.exp(buf[k] - top)
        acc = top + jnp.log(tot)
    o_ref[...] = acc


def combine(x, group, mode, cid):
    n = 1
    for _, size in group:
        n *= size
    size = x.shape[0]
    rows = size // 128
    x2 = x.reshape(rows, 128)
    out = pl.pallas_call(
        functools.partial(_combine_kernel, group, n, mode),
        out_shape=jax.ShapeDtypeStruct((rows, 128), jnp.float32),
        in_specs=[pl.BlockSpec(memory_space=pltpu.VMEM)],
        out_specs=pl.BlockSpec(memory_space=pltpu.VMEM),
        scratch_shapes=[
            pltpu.VMEM((n, rows, 128), jnp.float32),
            pltpu.SemaphoreType.DMA((n,)),
            pltpu.SemaphoreType.DMA((n,)),
        ],
        compiler_params=pltpu.CompilerParams(collective_id=cid, has_side_effects=True),
    )(x2)
    return out.reshape(size)

from jax.sharding import Mesh, PartitionSpec as P

ITERS = 3


SMOOTHING = 0.25


def gathered_lse(part, group, cid):
    return combine(part, group, "lse", cid)


def gathered_sum(part, group, cid):
    return combine(part, group, "sum", cid)


TM = 256
INV_EPS = 1.0 / SMOOTHING


def _scores_t(img_ref, cap_ref, inv_root):
    return lax.dot_general(
        cap_ref[...], img_ref[...], (((1,), (1,)), ((), ())), preferred_element_type=jnp.float32
    ) * inv_root


def _lane_chunks(x):
    return [x[:, k * 128:(k + 1) * 128] for k in range(x.shape[1] // 128)]


def _row_kernel(mode, inv_root, img_ref, cap_ref, a_ref, b_ref, w_ref, o_ref):
    s = _scores_t(img_ref, cap_ref, inv_root)
    if mode == "lse":
        x = (b_ref[...] + s) * INV_EPS
        top = jnp.max(x, axis=0, keepdims=True)
        o_ref[...] = top + jnp.log(jnp.sum(jnp.exp(x - top), axis=0, keepdims=True))
    else:
        plan = jnp.exp((a_ref[...] + s) * INV_EPS - b_ref[...])
        o_ref[...] = jnp.sum(plan * w_ref[...], axis=0, keepdims=True)


def _specs(n, c, e):
    return [
        pl.BlockSpec((TM, e), lambda i: (i, 0)),
        pl.BlockSpec((c, e), lambda i: (0, 0)),
        pl.BlockSpec((1, TM), lambda i: (0, i)),
        pl.BlockSpec((c, 1), lambda i: (0, 0)),
    ]


def row_pass(mode, images, captions, a, b, w):
    n, e = images.shape
    c = captions.shape[0]
    inv_root = 1.0 / math.sqrt(e)
    out = pl.pallas_call(
        functools.partial(_row_kernel, mode, inv_root),
        out_shape=jax.ShapeDtypeStruct((1, n), jnp.float32),
        grid=(n // TM,),
        in_specs=_specs(n, c, e) + [pl.BlockSpec((c, 1), lambda i: (0, 0))],
        out_specs=pl.BlockSpec((1, TM), lambda i: (0, i)),
        cost_estimate=pl.CostEstimate(
            flops=2 * n * c * e, transcendentals=n * c, bytes_accessed=n * e * 2 + c * e * 2
        ),
    )(images, captions, a.reshape(1, n), b.reshape(c, 1), w.reshape(c, 1))
    return out.reshape(n)


def _col_kernel(mode, inv_root, img_ref, cap_ref, a_ref, b_ref, w_ref, o_ref, top_ref, tot_ref):
    step = pl.program_id(0)
    s = _scores_t(img_ref, cap_ref, inv_root)
    if mode == "lse":
        chunks = _lane_chunks((a_ref[...] + s) * INV_EPS)

        @pl.when(step == 0)
        def _():
            top_ref[...] = jnp.full(top_ref.shape, -jnp.inf, jnp.float32)
            tot_ref[...] = jnp.zeros(tot_ref.shape, jnp.float32)

        cmax = chunks[0]
        for piece in chunks[1:]:
            cmax = jnp.maximum(cmax, piece)
        old = top_ref[...]
        top = jnp.maximum(old, cmax)
        tot = tot_ref[...] * jnp.exp(old - top)
        for piece in chunks:
            tot = tot + jnp.exp(piece - top)
        tot_ref[...] = tot
        top_ref[...] = top

        @pl.when(step == pl.num_programs(0) - 1)
        def _():
            t = top_ref[...]
            m = jnp.max(t, axis=1, keepdims=True)
            o_ref[...] = m + jnp.log(jnp.sum(tot_ref[...] * jnp.exp(t - m), axis=1, keepdims=True))
    else:
        plan = jnp.exp((b_ref[...] + s) * INV_EPS - a_ref[...])
        chunks = _lane_chunks(plan * w_ref[...])

        @pl.when(step == 0)
        def _():
            tot_ref[...] = jnp.zeros(tot_ref.shape, jnp.float32)

        acc = chunks[0]
        for piece in chunks[1:]:
            acc = acc + piece
        tot_ref[...] += acc

        @pl.when(step == pl.num_programs(0) - 1)
        def _():
            o_ref[...] = jnp.sum(tot_ref[...], axis=1, keepdims=True)


def col_pass(mode, images, captions, a, w, b):
    n, e = images.shape
    c = captions.shape[0]
    inv_root = 1.0 / math.sqrt(e)
    out = pl.pallas_call(
        functools.partial(_col_kernel, mode, inv_root),
        out_shape=jax.ShapeDtypeStruct((c, 1), jnp.float32),
        grid=(n // TM,),
        in_specs=_specs(n, c, e) + [pl.BlockSpec((1, TM), lambda i: (0, i))],
        out_specs=pl.BlockSpec((c, 1), lambda i: (0, 0)),
        scratch_shapes=[pltpu.VMEM((c, 128), jnp.float32), pltpu.VMEM((c, 128), jnp.float32)],
        cost_estimate=pl.CostEstimate(
            flops=2 * n * c * e, transcendentals=n * c, bytes_accessed=n * e * 2 + c * e * 2
        ),
    )(images, captions, a.reshape(1, n), b.reshape(c, 1), w.reshape(1, n))
    return out.reshape(c)


def _final_kernel(inv_root, img_ref, cap_ref, rows_ref, cols_ref, ig_ref, cg_ref):
    step = pl.program_id(0)
    s = _scores_t(img_ref, cap_ref, inv_root)
    rows = rows_ref[...]
    cols = cols_ref[...]
    logw_r = rows[6:7, :]
    logw_c = cols[:, 7:8]
    adjoint = jnp.zeros(s.shape, jnp.float32)
    for level in reversed(range(ITERS)):
        f = rows[level:level + 1, :]
        fb = rows[3 + level:4 + level, :]
        g_prev = cols[:, level:level + 1]
        g = cols[:, level + 1:level + 2]
        gb = cols[:, 4 + level:5 + level]
        col_plan = jnp.exp((f + s) * INV_EPS - (logw_c - g * INV_EPS))
        adjoint = adjoint - col_plan * gb
        row_plan = jnp.exp((g_prev + s) * INV_EPS - (logw_r - f * INV_EPS))
        adjoint = adjoint - row_plan * fb
    rounded = adjoint.astype(jnp.bfloat16)
    ig_ref[...] = lax.dot_general(
        rounded, cap_ref[...], (((0,), (0,)), ((), ())), preferred_element_type=jnp.float32
    ) * inv_root

    @pl.when(step == 0)
    def _():
        cg_ref[...] = jnp.zeros(cg_ref.shape, jnp.float32)

    cg_ref[...] += jnp.dot(rounded, img_ref[...], preferred_element_type=jnp.float32) * inv_root


def final_pass(images, captions, rows, cols):
    n, e = images.shape
    c = captions.shape[0]
    inv_root = 1.0 / math.sqrt(e)
    return pl.pallas_call(
        functools.partial(_final_kernel, inv_root),
        out_shape=(
            jax.ShapeDtypeStruct((n, e), jnp.float32),
            jax.ShapeDtypeStruct((c, e), jnp.float32),
        ),
        grid=(n // TM,),
        in_specs=[
            pl.BlockSpec((TM, e), lambda i: (i, 0)),
            pl.BlockSpec((c, e), lambda i: (0, 0)),
            pl.BlockSpec((8, TM), lambda i: (0, i)),
            pl.BlockSpec((c, 8), lambda i: (0, 0)),
        ],
        out_specs=(
            pl.BlockSpec((TM, e), lambda i: (i, 0)),
            pl.BlockSpec((c, e), lambda i: (0, 0)),
        ),
        cost_estimate=pl.CostEstimate(
            flops=6 * n * c * e, transcendentals=6 * n * c, bytes_accessed=n * e * 6 + c * e * 6
        ),
    )(images, captions, rows, cols)


def body(images, captions, image_logw, caption_logw, image_cot, caption_cot, *, n_img, ny, nx):
    rows_here = images.shape[0] // ny
    start = lax.axis_index("cy") * rows_here
    images = lax.dynamic_slice_in_dim(images, start, rows_here, 0)
    image_logw = lax.dynamic_slice_in_dim(image_logw, start, rows_here, 0)
    image_cot = lax.dynamic_slice_in_dim(image_cot, start, rows_here, 0)
    captions = lax.all_gather(captions, "cy", tiled=True)
    vecs = lax.all_gather(jnp.stack([caption_logw, caption_cot]), "cy", axis=1, tiled=True)
    caption_logw = vecs[0]
    caption_cot = vecs[1]
    row_group = (("cx", nx),)
    col_group = (("cy", ny), ("img", n_img))
    n = images.shape[0]
    c = captions.shape[0]
    zeros_r = jnp.zeros((n,), jnp.float32)
    zeros_c = jnp.zeros((c,), jnp.float32)
    col_hist = [zeros_c]
    row_hist = []
    for level in range(ITERS):
        part = row_pass("lse", images, captions, zeros_r, col_hist[-1], zeros_c)
        row_pot = SMOOTHING * image_logw - SMOOTHING * gathered_lse(part, row_group, 0)
        row_hist.append(row_pot)
        part = col_pass("lse", images, captions, row_pot, zeros_r, zeros_c)
        col_hist.append(SMOOTHING * caption_logw - SMOOTHING * gathered_lse(part, col_group, 1))
    col_bar = caption_cot
    row_bars = [None] * ITERS
    col_bars = [None] * ITERS
    for level in reversed(range(ITERS)):
        col_bars[level] = col_bar
        shift_col = caption_logw - col_hist[level + 1] / SMOOTHING
        part = row_pass("wsum", images, captions, row_hist[level], shift_col, col_bar)
        row_bar = -gathered_sum(part, row_group, 2)
        if level == ITERS - 1:
            row_bar = image_cot + row_bar
        row_bars[level] = row_bar
        if level > 0:
            shift_row = image_logw - row_hist[level] / SMOOTHING
            part = col_pass("wsum", images, captions, shift_row, row_bar, col_hist[level])
            col_bar = -gathered_sum(part, col_group, 3)
    rows = jnp.stack(row_hist + row_bars + [image_logw, zeros_r], axis=0)
    cols = jnp.stack(col_hist + col_bars + [caption_logw], axis=1)
    ig_part, cg_part = final_pass(images, captions, rows, cols)
    image_grad = lax.psum_scatter(ig_part, "cx", scatter_dimension=0, tiled=True)
    caption_grad = lax.psum_scatter(cg_part, ("cy", "img"), scatter_dimension=0, tiled=True)
    return (image_grad, caption_grad)


def solution(mesh):
    n_img = mesh.shape["img"]
    n_cap = mesh.shape["cap"]
    nx = int(math.isqrt(n_cap))
    while n_cap % nx:
        nx -= 1
    ny = n_cap // nx
    grid = Mesh(mesh.devices.reshape(n_img, ny, nx), AXES)
    in_specs = (
        P("img", None),
        P(("cy", "cx"), None),
        P("img"),
        P(("cy", "cx")),
        P("img"),
        P(("cy", "cx")),
    )
    out_specs = (P(("img", "cy", "cx"), None), P(("cy", "cx", "img"), None))
    return jax.shard_map(
        functools.partial(body, n_img=n_img, ny=ny, nx=nx),
        mesh=grid,
        in_specs=in_specs,
        out_specs=out_specs,
        check_vma=False,
    )
```

```python
import functools
import math

import jax
import jax.numpy as jnp
from jax import lax
from jax.experimental import pallas as pl
from jax.experimental.pallas import tpu as pltpu

MESH = pl.DeviceIdType.MESH
AXES = ("img", "cy", "cx")


def _peer(group, k):
    idx = {name: lax.axis_index(name) for name in AXES}
    total = 1
    lin = 0
    for name, size in group:
        lin = lin * size + idx[name]
        total *= size
    lin = lax.rem(lin + k, total)
    for name, size in reversed(group):
        idx[name] = lax.rem(lin, size)
        lin = lin // size
    return tuple(idx[name] for name in AXES)


def _combine_kernel(group, n, mode, x_ref, o_ref, buf, send_sem, recv_sem):
    barrier = pltpu.get_barrier_semaphore()
    for k in range(1, n):
        pl.semaphore_signal(barrier, inc=1, device_id=_peer(group, k), device_id_type=MESH)
    pl.semaphore_wait(barrier, n - 1)
    copies = []
    for k in range(1, n):
        copy = pltpu.make_async_remote_copy(
            src_ref=x_ref,
            dst_ref=buf.at[k],
            send_sem=send_sem.at[k],
            recv_sem=recv_sem.at[k],
            device_id=_peer(group, k),
            device_id_type=MESH,
        )
        copy.start()
        copies.append(copy)
    for copy in copies:
        copy.wait()
    x = x_ref[...]
    if mode == "sum":
        acc = x
        for k in range(1, n):
            acc = acc + buf[k]
    else:
        top = x
        for k in range(1, n):
            top = jnp.maximum(top, buf[k])
        tot = jnp.exp(x - top)
        for k in range(1, n):
            tot = tot + jnp.exp(buf[k] - top)
        acc = top + jnp.log(tot)
    o_ref[...] = acc


def combine(x, group, mode, cid):
    n = 1
    for _, size in group:
        n *= size
    size = x.shape[0]
    rows = size // 128
    x2 = x.reshape(rows, 128)
    out = pl.pallas_call(
        functools.partial(_combine_kernel, group, n, mode),
        out_shape=jax.ShapeDtypeStruct((rows, 128), jnp.float32),
        in_specs=[pl.BlockSpec(memory_space=pltpu.VMEM)],
        out_specs=pl.BlockSpec(memory_space=pltpu.VMEM),
        scratch_shapes=[
            pltpu.VMEM((n, rows, 128), jnp.float32),
            pltpu.SemaphoreType.DMA((n,)),
            pltpu.SemaphoreType.DMA((n,)),
        ],
        compiler_params=pltpu.CompilerParams(collective_id=cid, has_side_effects=True),
    )(x2)
    return out.reshape(size)

from jax.sharding import Mesh, PartitionSpec as P

ITERS = 3


SMOOTHING = 0.25


def gathered_lse(part, group, cid):
    return combine(part, group, "lse", cid)


def gathered_sum(part, group, cid):
    return combine(part, group, "sum", cid)


TM = 256
INV_EPS = 1.0 / SMOOTHING


def _scores_t(img_ref, cap_ref, inv_root):
    return lax.dot_general(
        cap_ref[...], img_ref[...], (((1,), (1,)), ((), ())), preferred_element_type=jnp.float32
    ) * inv_root


def _lane_chunks(x):
    return [x[:, k * 128:(k + 1) * 128] for k in range(x.shape[1] // 128)]


def _row_kernel(mode, inv_root, img_ref, cap_ref, a_ref, b_ref, w_ref, o_ref):
    s = _scores_t(img_ref, cap_ref, inv_root)
    if mode == "lse":
        x = (b_ref[...] + s) * INV_EPS
        top = jnp.max(x, axis=0, keepdims=True)
        o_ref[...] = top + jnp.log(jnp.sum(jnp.exp(x - top), axis=0, keepdims=True))
    else:
        plan = jnp.exp((a_ref[...] + s) * INV_EPS - b_ref[...])
        o_ref[...] = jnp.sum(plan * w_ref[...], axis=0, keepdims=True)


def _specs(n, c, e):
    return [
        pl.BlockSpec((TM, e), lambda i: (i, 0)),
        pl.BlockSpec((c, e), lambda i: (0, 0)),
        pl.BlockSpec((1, TM), lambda i: (0, i)),
        pl.BlockSpec((c, 1), lambda i: (0, 0)),
    ]


def row_pass(mode, images, captions, a, b, w):
    n, e = images.shape
    c = captions.shape[0]
    inv_root = 1.0 / math.sqrt(e)
    out = pl.pallas_call(
        functools.partial(_row_kernel, mode, inv_root),
        out_shape=jax.ShapeDtypeStruct((1, n), jnp.float32),
        grid=(n // TM,),
        in_specs=_specs(n, c, e) + [pl.BlockSpec((c, 1), lambda i: (0, 0))],
        out_specs=pl.BlockSpec((1, TM), lambda i: (0, i)),
        cost_estimate=pl.CostEstimate(
            flops=2 * n * c * e, transcendentals=n * c, bytes_accessed=n * e * 2 + c * e * 2
        ),
    )(images, captions, a.reshape(1, n), b.reshape(c, 1), w.reshape(c, 1))
    return out.reshape(n)


def _col_kernel(mode, inv_root, img_ref, cap_ref, a_ref, b_ref, w_ref, o_ref, top_ref, tot_ref):
    step = pl.program_id(0)
    s = _scores_t(img_ref, cap_ref, inv_root)
    if mode == "lse":
        chunks = _lane_chunks((a_ref[...] + s) * INV_EPS)

        @pl.when(step == 0)
        def _():
            top_ref[...] = jnp.full(top_ref.shape, -jnp.inf, jnp.float32)
            tot_ref[...] = jnp.zeros(tot_ref.shape, jnp.float32)

        cmax = chunks[0]
        for piece in chunks[1:]:
            cmax = jnp.maximum(cmax, piece)
        old = top_ref[...]
        top = jnp.maximum(old, cmax)
        tot = tot_ref[...] * jnp.exp(old - top)
        for piece in chunks:
            tot = tot + jnp.exp(piece - top)
        tot_ref[...] = tot
        top_ref[...] = top

        @pl.when(step == pl.num_programs(0) - 1)
        def _():
            t = top_ref[...]
            m = jnp.max(t, axis=1, keepdims=True)
            o_ref[...] = m + jnp.log(jnp.sum(tot_ref[...] * jnp.exp(t - m), axis=1, keepdims=True))
    else:
        plan = jnp.exp((b_ref[...] + s) * INV_EPS - a_ref[...])
        chunks = _lane_chunks(plan * w_ref[...])

        @pl.when(step == 0)
        def _():
            tot_ref[...] = jnp.zeros(tot_ref.shape, jnp.float32)

        acc = chunks[0]
        for piece in chunks[1:]:
            acc = acc + piece
        tot_ref[...] += acc

        @pl.when(step == pl.num_programs(0) - 1)
        def _():
            o_ref[...] = jnp.sum(tot_ref[...], axis=1, keepdims=True)


def col_pass(mode, images, captions, a, w, b):
    n, e = images.shape
    c = captions.shape[0]
    inv_root = 1.0 / math.sqrt(e)
    out = pl.pallas_call(
        functools.partial(_col_kernel, mode, inv_root),
        out_shape=jax.ShapeDtypeStruct((c, 1), jnp.float32),
        grid=(n // TM,),
        in_specs=_specs(n, c, e) + [pl.BlockSpec((1, TM), lambda i: (0, i))],
        out_specs=pl.BlockSpec((c, 1), lambda i: (0, 0)),
        scratch_shapes=[pltpu.VMEM((c, 128), jnp.float32), pltpu.VMEM((c, 128), jnp.float32)],
        cost_estimate=pl.CostEstimate(
            flops=2 * n * c * e, transcendentals=n * c, bytes_accessed=n * e * 2 + c * e * 2
        ),
    )(images, captions, a.reshape(1, n), b.reshape(c, 1), w.reshape(1, n))
    return out.reshape(c)


def _final_kernel(inv_root, img_ref, cap_ref, rows_ref, cols_ref, ig_ref, cg_ref):
    step = pl.program_id(0)
    s = _scores_t(img_ref, cap_ref, inv_root)
    rows = rows_ref[...]
    cols = cols_ref[...]
    logw_r = rows[6:7, :]
    logw_c = cols[:, 7:8]
    adjoint = jnp.zeros(s.shape, jnp.float32)
    for level in reversed(range(ITERS)):
        f = rows[level:level + 1, :]
        fb = rows[3 + level:4 + level, :]
        g_prev = cols[:, level:level + 1]
        g = cols[:, level + 1:level + 2]
        gb = cols[:, 4 + level:5 + level]
        col_plan = jnp.exp((f + s) * INV_EPS - (logw_c - g * INV_EPS))
        adjoint = adjoint - col_plan * gb
        row_plan = jnp.exp((g_prev + s) * INV_EPS - (logw_r - f * INV_EPS))
        adjoint = adjoint - row_plan * fb
    rounded = adjoint.astype(jnp.bfloat16)
    ig_ref[...] = lax.dot_general(
        rounded, cap_ref[...], (((0,), (0,)), ((), ())), preferred_element_type=jnp.float32
    ) * inv_root

    @pl.when(step == 0)
    def _():
        cg_ref[...] = jnp.zeros(cg_ref.shape, jnp.float32)

    cg_ref[...] += jnp.dot(rounded, img_ref[...], preferred_element_type=jnp.float32) * inv_root


def final_pass(images, captions, rows, cols):
    n, e = images.shape
    c = captions.shape[0]
    inv_root = 1.0 / math.sqrt(e)
    return pl.pallas_call(
        functools.partial(_final_kernel, inv_root),
        out_shape=(
            jax.ShapeDtypeStruct((n, e), jnp.float32),
            jax.ShapeDtypeStruct((c, e), jnp.float32),
        ),
        grid=(n // TM,),
        in_specs=[
            pl.BlockSpec((TM, e), lambda i: (i, 0)),
            pl.BlockSpec((c, e), lambda i: (0, 0)),
            pl.BlockSpec((8, TM), lambda i: (0, i)),
            pl.BlockSpec((c, 8), lambda i: (0, 0)),
        ],
        out_specs=(
            pl.BlockSpec((TM, e), lambda i: (i, 0)),
            pl.BlockSpec((c, e), lambda i: (0, 0)),
        ),
        cost_estimate=pl.CostEstimate(
            flops=6 * n * c * e, transcendentals=6 * n * c, bytes_accessed=n * e * 6 + c * e * 6
        ),
    )(images, captions, rows, cols)


def body(images, captions, image_logw, caption_logw, image_cot, caption_cot, *, n_img, ny, nx):
    rows_here = images.shape[0] // ny
    start = lax.axis_index("cy") * rows_here
    images = lax.dynamic_slice_in_dim(images, start, rows_here, 0)
    image_logw = lax.dynamic_slice_in_dim(image_logw, start, rows_here, 0)
    image_cot = lax.dynamic_slice_in_dim(image_cot, start, rows_here, 0)
    e = captions.shape[1]
    joined = jnp.concatenate(
        [captions.astype(jnp.float32), jnp.stack([caption_logw, caption_cot], axis=1)], axis=1
    )
    joined = lax.all_gather(joined, "cy", tiled=True)
    captions = joined[:, :e].astype(jnp.bfloat16)
    caption_logw = joined[:, e]
    caption_cot = joined[:, e + 1]
    row_group = (("cx", nx),)
    col_group = (("cy", ny), ("img", n_img))
    n = images.shape[0]
    c = captions.shape[0]
    zeros_r = jnp.zeros((n,), jnp.float32)
    zeros_c = jnp.zeros((c,), jnp.float32)
    col_hist = [zeros_c]
    row_hist = []
    for level in range(ITERS):
        part = row_pass("lse", images, captions, zeros_r, col_hist[-1], zeros_c)
        row_pot = SMOOTHING * image_logw - SMOOTHING * gathered_lse(part, row_group, 0)
        row_hist.append(row_pot)
        part = col_pass("lse", images, captions, row_pot, zeros_r, zeros_c)
        col_hist.append(SMOOTHING * caption_logw - SMOOTHING * gathered_lse(part, col_group, 1))
    col_bar = caption_cot
    row_bars = [None] * ITERS
    col_bars = [None] * ITERS
    for level in reversed(range(ITERS)):
        col_bars[level] = col_bar
        shift_col = caption_logw - col_hist[level + 1] / SMOOTHING
        part = row_pass("wsum", images, captions, row_hist[level], shift_col, col_bar)
        row_bar = -gathered_sum(part, row_group, 2)
        if level == ITERS - 1:
            row_bar = image_cot + row_bar
        row_bars[level] = row_bar
        if level > 0:
            shift_row = image_logw - row_hist[level] / SMOOTHING
            part = col_pass("wsum", images, captions, shift_row, row_bar, col_hist[level])
            col_bar = -gathered_sum(part, col_group, 3)
    rows = jnp.stack(row_hist + row_bars + [image_logw, zeros_r], axis=0)
    cols = jnp.stack(col_hist + col_bars + [caption_logw], axis=1)
    ig_part, cg_part = final_pass(images, captions, rows, cols)
    image_grad = lax.psum_scatter(ig_part, "cx", scatter_dimension=0, tiled=True)
    piece = c // (ny * n_img)
    staged = cg_part.reshape(ny, n_img, piece, e).transpose(1, 0, 2, 3).reshape(c, e)
    staged = lax.psum_scatter(staged, "img", scatter_dimension=0, tiled=True)
    caption_grad = lax.psum_scatter(staged, "cy", scatter_dimension=0, tiled=True)
    return (image_grad, caption_grad)


def solution(mesh):
    n_img = mesh.shape["img"]
    n_cap = mesh.shape["cap"]
    nx = int(math.isqrt(n_cap))
    while n_cap % nx:
        nx -= 1
    ny = n_cap // nx
    grid = Mesh(mesh.devices.reshape(n_img, ny, nx), AXES)
    in_specs = (
        P("img", None),
        P(("cy", "cx"), None),
        P("img"),
        P(("cy", "cx")),
        P("img"),
        P(("cy", "cx")),
    )
    out_specs = (P(("img", "cy", "cx"), None), P(("cy", "cx", "img"), None))
    return jax.shard_map(
        functools.partial(body, n_img=n_img, ny=ny, nx=nx),
        mesh=grid,
        in_specs=in_specs,
        out_specs=out_specs,
        check_vma=False,
    )
```

```python
import functools
import math

import jax
import jax.numpy as jnp
from jax import lax
from jax.experimental import pallas as pl
from jax.experimental.pallas import tpu as pltpu

MESH = pl.DeviceIdType.MESH


def _peer(axis, k, n):
    me_img = lax.axis_index("img")
    me_cap = lax.axis_index("cap")
    if axis == "cap":
        return (me_img, lax.rem(me_cap + k, n))
    return (lax.rem(me_img + k, n), me_cap)


def _combine_kernel(axis, n, mode, x_ref, o_ref, buf, send_sem, recv_sem):
    barrier = pltpu.get_barrier_semaphore()
    for k in range(1, n):
        pl.semaphore_signal(barrier, inc=1, device_id=_peer(axis, k, n), device_id_type=MESH)
    pl.semaphore_wait(barrier, n - 1)
    copies = []
    for k in range(1, n):
        copy = pltpu.make_async_remote_copy(
            src_ref=x_ref,
            dst_ref=buf.at[k],
            send_sem=send_sem.at[k],
            recv_sem=recv_sem.at[k],
            device_id=_peer(axis, k, n),
            device_id_type=MESH,
        )
        copy.start()
        copies.append(copy)
    for copy in copies:
        copy.wait()
    x = x_ref[...]
    if mode == "sum":
        acc = x
        for k in range(1, n):
            acc = acc + buf[k]
    else:
        top = x
        for k in range(1, n):
            top = jnp.maximum(top, buf[k])
        tot = jnp.exp(x - top)
        for k in range(1, n):
            tot = tot + jnp.exp(buf[k] - top)
        acc = top + jnp.log(tot)
    o_ref[...] = acc


def combine(x, axis, n, mode, cid):
    size = x.shape[0]
    rows = size // 128
    x2 = x.reshape(rows, 128)
    out = pl.pallas_call(
        functools.partial(_combine_kernel, axis, n, mode),
        out_shape=jax.ShapeDtypeStruct((rows, 128), jnp.float32),
        in_specs=[pl.BlockSpec(memory_space=pltpu.VMEM)],
        out_specs=pl.BlockSpec(memory_space=pltpu.VMEM),
        scratch_shapes=[
            pltpu.VMEM((n, rows, 128), jnp.float32),
            pltpu.SemaphoreType.DMA((n,)),
            pltpu.SemaphoreType.DMA((n,)),
        ],
        compiler_params=pltpu.CompilerParams(collective_id=cid, has_side_effects=True),
    )(x2)
    return out.reshape(size)

from jax.sharding import PartitionSpec as P

ITERS = 3


SMOOTHING = 0.25


_IDS = {("cap", "lse"): 0, ("img", "lse"): 1, ("cap", "sum"): 2, ("img", "sum"): 3}


def gathered_lse(part, axis):
    return combine(part, axis, lax.axis_size(axis), "lse", _IDS[(axis, "lse")])


def gathered_sum(part, axis):
    return combine(part, axis, lax.axis_size(axis), "sum", _IDS[(axis, "sum")])


TM = 1024
INV_EPS = 1.0 / SMOOTHING


def _scores_t(img_ref, cap_ref, inv_root):
    return lax.dot_general(
        cap_ref[...], img_ref[...], (((1,), (1,)), ((), ())), preferred_element_type=jnp.float32
    ) * inv_root


def _lane_chunks(x):
    return [x[:, k * 128:(k + 1) * 128] for k in range(x.shape[1] // 128)]


def _row_kernel(mode, inv_root, img_ref, cap_ref, a_ref, b_ref, w_ref, o_ref):
    s = _scores_t(img_ref, cap_ref, inv_root)
    if mode == "lse":
        x = (b_ref[...] + s) * INV_EPS
        top = jnp.max(x, axis=0, keepdims=True)
        o_ref[...] = top + jnp.log(jnp.sum(jnp.exp(x - top), axis=0, keepdims=True))
    else:
        plan = jnp.exp((a_ref[...] + s) * INV_EPS - b_ref[...])
        o_ref[...] = jnp.sum(plan * w_ref[...], axis=0, keepdims=True)


def _specs(n, c, e):
    return [
        pl.BlockSpec((TM, e), lambda i: (i, 0)),
        pl.BlockSpec((c, e), lambda i: (0, 0)),
        pl.BlockSpec((1, TM), lambda i: (0, i)),
        pl.BlockSpec((c, 1), lambda i: (0, 0)),
    ]


def row_pass(mode, images, captions, a, b, w):
    n, e = images.shape
    c = captions.shape[0]
    inv_root = 1.0 / math.sqrt(e)
    out = pl.pallas_call(
        functools.partial(_row_kernel, mode, inv_root),
        out_shape=jax.ShapeDtypeStruct((1, n), jnp.float32),
        grid=(n // TM,),
        in_specs=_specs(n, c, e) + [pl.BlockSpec((c, 1), lambda i: (0, 0))],
        out_specs=pl.BlockSpec((1, TM), lambda i: (0, i)),
        cost_estimate=pl.CostEstimate(
            flops=2 * n * c * e, transcendentals=n * c, bytes_accessed=n * e * 2 + c * e * 2
        ),
    )(images, captions, a.reshape(1, n), b.reshape(c, 1), w.reshape(c, 1))
    return out.reshape(n)


def _col_kernel(mode, inv_root, img_ref, cap_ref, a_ref, b_ref, w_ref, o_ref, top_ref, tot_ref):
    step = pl.program_id(0)
    s = _scores_t(img_ref, cap_ref, inv_root)
    if mode == "lse":
        chunks = _lane_chunks((a_ref[...] + s) * INV_EPS)

        @pl.when(step == 0)
        def _():
            top_ref[...] = jnp.full(top_ref.shape, -jnp.inf, jnp.float32)
            tot_ref[...] = jnp.zeros(tot_ref.shape, jnp.float32)

        cmax = chunks[0]
        for piece in chunks[1:]:
            cmax = jnp.maximum(cmax, piece)
        old = top_ref[...]
        top = jnp.maximum(old, cmax)
        tot = tot_ref[...] * jnp.exp(old - top)
        for piece in chunks:
            tot = tot + jnp.exp(piece - top)
        tot_ref[...] = tot
        top_ref[...] = top

        @pl.when(step == pl.num_programs(0) - 1)
        def _():
            t = top_ref[...]
            m = jnp.max(t, axis=1, keepdims=True)
            o_ref[...] = m + jnp.log(jnp.sum(tot_ref[...] * jnp.exp(t - m), axis=1, keepdims=True))
    else:
        plan = jnp.exp((b_ref[...] + s) * INV_EPS - a_ref[...])
        chunks = _lane_chunks(plan * w_ref[...])

        @pl.when(step == 0)
        def _():
            tot_ref[...] = jnp.zeros(tot_ref.shape, jnp.float32)

        acc = chunks[0]
        for piece in chunks[1:]:
            acc = acc + piece
        tot_ref[...] += acc

        @pl.when(step == pl.num_programs(0) - 1)
        def _():
            o_ref[...] = jnp.sum(tot_ref[...], axis=1, keepdims=True)


def col_pass(mode, images, captions, a, w, b):
    n, e = images.shape
    c = captions.shape[0]
    inv_root = 1.0 / math.sqrt(e)
    out = pl.pallas_call(
        functools.partial(_col_kernel, mode, inv_root),
        out_shape=jax.ShapeDtypeStruct((c, 1), jnp.float32),
        grid=(n // TM,),
        in_specs=_specs(n, c, e) + [pl.BlockSpec((1, TM), lambda i: (0, i))],
        out_specs=pl.BlockSpec((c, 1), lambda i: (0, 0)),
        scratch_shapes=[pltpu.VMEM((c, 128), jnp.float32), pltpu.VMEM((c, 128), jnp.float32)],
        cost_estimate=pl.CostEstimate(
            flops=2 * n * c * e, transcendentals=n * c, bytes_accessed=n * e * 2 + c * e * 2
        ),
    )(images, captions, a.reshape(1, n), b.reshape(c, 1), w.reshape(1, n))
    return out.reshape(c)


def _final_kernel(inv_root, img_ref, cap_ref, rows_ref, cols_ref, ig_ref, cg_ref):
    step = pl.program_id(0)
    s = _scores_t(img_ref, cap_ref, inv_root)
    rows = rows_ref[...]
    cols = cols_ref[...]
    logw_r = rows[6:7, :]
    logw_c = cols[:, 7:8]
    adjoint = jnp.zeros(s.shape, jnp.float32)
    for level in reversed(range(ITERS)):
        f = rows[level:level + 1, :]
        fb = rows[3 + level:4 + level, :]
        g_prev = cols[:, level:level + 1]
        g = cols[:, level + 1:level + 2]
        gb = cols[:, 4 + level:5 + level]
        col_plan = jnp.exp((f + s) * INV_EPS - (logw_c - g * INV_EPS))
        adjoint = adjoint - col_plan * gb
        row_plan = jnp.exp((g_prev + s) * INV_EPS - (logw_r - f * INV_EPS))
        adjoint = adjoint - row_plan * fb
    rounded = adjoint.astype(jnp.bfloat16)
    ig_ref[...] = lax.dot_general(
        rounded, cap_ref[...], (((0,), (0,)), ((), ())), preferred_element_type=jnp.float32
    ) * inv_root

    @pl.when(step == 0)
    def _():
        cg_ref[...] = jnp.zeros(cg_ref.shape, jnp.float32)

    cg_ref[...] += jnp.dot(rounded, img_ref[...], preferred_element_type=jnp.float32) * inv_root


def final_pass(images, captions, rows, cols):
    n, e = images.shape
    c = captions.shape[0]
    inv_root = 1.0 / math.sqrt(e)
    return pl.pallas_call(
        functools.partial(_final_kernel, inv_root),
        out_shape=(
            jax.ShapeDtypeStruct((n, e), jnp.float32),
            jax.ShapeDtypeStruct((c, e), jnp.float32),
        ),
        grid=(n // TM,),
        in_specs=[
            pl.BlockSpec((TM, e), lambda i: (i, 0)),
            pl.BlockSpec((c, e), lambda i: (0, 0)),
            pl.BlockSpec((8, TM), lambda i: (0, i)),
            pl.BlockSpec((c, 8), lambda i: (0, 0)),
        ],
        out_specs=(
            pl.BlockSpec((TM, e), lambda i: (i, 0)),
            pl.BlockSpec((c, e), lambda i: (0, 0)),
        ),
        cost_estimate=pl.CostEstimate(
            flops=6 * n * c * e, transcendentals=6 * n * c, bytes_accessed=n * e * 6 + c * e * 6
        ),
    )(images, captions, rows, cols)


CHUNKS = 2


def _interleave(x, owners):
    rest = x.shape[1:]
    x = x.reshape((owners, CHUNKS, x.shape[0] // (owners * CHUNKS)) + rest)
    return jnp.swapaxes(x, 0, 1).reshape((-1,) + rest)


def body(images, captions, image_logw, caption_logw, image_cot, caption_cot):
    owners = lax.axis_size("cap")
    images = _interleave(images, owners)
    image_logw = _interleave(image_logw, owners)
    image_cot = _interleave(image_cot, owners)
    n = images.shape[0]
    c = captions.shape[0]
    zeros_r = jnp.zeros((n,), jnp.float32)
    zeros_c = jnp.zeros((c,), jnp.float32)
    col_hist = [zeros_c]
    row_hist = []
    for level in range(ITERS):
        part = row_pass("lse", images, captions, zeros_r, col_hist[-1], zeros_c)
        row_pot = SMOOTHING * image_logw - SMOOTHING * gathered_lse(part, "cap")
        row_hist.append(row_pot)
        part = col_pass("lse", images, captions, row_pot, zeros_r, zeros_c)
        col_hist.append(SMOOTHING * caption_logw - SMOOTHING * gathered_lse(part, "img"))
    col_bar = caption_cot
    row_bars = [None] * ITERS
    col_bars = [None] * ITERS
    for level in reversed(range(ITERS)):
        col_bars[level] = col_bar
        shift_col = caption_logw - col_hist[level + 1] / SMOOTHING
        part = row_pass("wsum", images, captions, row_hist[level], shift_col, col_bar)
        row_bar = -gathered_sum(part, "cap")
        if level == ITERS - 1:
            row_bar = image_cot + row_bar
        row_bars[level] = row_bar
        if level > 0:
            shift_row = image_logw - row_hist[level] / SMOOTHING
            part = col_pass("wsum", images, captions, shift_row, row_bar, col_hist[level])
            col_bar = -gathered_sum(part, "img")
    rows = jnp.stack(row_hist + row_bars + [image_logw, zeros_r], axis=0)
    cols = jnp.stack(col_hist + col_bars + [caption_logw], axis=1)
    span = n // CHUNKS
    grads = []
    cg_total = None
    for h in range(CHUNKS):
        ig_part, cg_part = final_pass(
            images[h * span:(h + 1) * span], captions, rows[:, h * span:(h + 1) * span], cols
        )
        grads.append(lax.psum_scatter(ig_part, "cap", scatter_dimension=0, tiled=True))
        cg_total = cg_part if cg_total is None else cg_total + cg_part
    image_grad = jnp.concatenate(grads, axis=0)
    caption_grad = lax.psum_scatter(cg_total, "img", scatter_dimension=0, tiled=True)
    return (image_grad, caption_grad)


def solution(mesh):
    in_specs = (P("img", None), P("cap", None), P("img"), P("cap"), P("img"), P("cap"))
    out_specs = (P(("img", "cap"), None), P(("cap", "img"), None))
    return jax.shard_map(body, mesh=mesh, in_specs=in_specs, out_specs=out_specs, check_vma=False)
```

```python
import functools
import math

import jax
import jax.numpy as jnp
from jax import lax
from jax.experimental import pallas as pl
from jax.experimental.pallas import tpu as pltpu

MESH = pl.DeviceIdType.MESH


def _peer(axis, k, n):
    me_img = lax.axis_index("img")
    me_cap = lax.axis_index("cap")
    if axis == "cap":
        return (me_img, lax.rem(me_cap + k, n))
    return (lax.rem(me_img + k, n), me_cap)


def _combine_kernel(axis, n, mode, x_ref, o_ref, buf, send_sem, recv_sem):
    barrier = pltpu.get_barrier_semaphore()
    for k in range(1, n):
        pl.semaphore_signal(barrier, inc=1, device_id=_peer(axis, k, n), device_id_type=MESH)
    pl.semaphore_wait(barrier, n - 1)
    copies = []
    for k in range(1, n):
        copy = pltpu.make_async_remote_copy(
            src_ref=x_ref,
            dst_ref=buf.at[k],
            send_sem=send_sem.at[k],
            recv_sem=recv_sem.at[k],
            device_id=_peer(axis, k, n),
            device_id_type=MESH,
        )
        copy.start()
        copies.append(copy)
    for copy in copies:
        copy.wait()
    x = x_ref[...]
    if mode == "sum":
        acc = x
        for k in range(1, n):
            acc = acc + buf[k]
    else:
        top = x
        for k in range(1, n):
            top = jnp.maximum(top, buf[k])
        tot = jnp.exp(x - top)
        for k in range(1, n):
            tot = tot + jnp.exp(buf[k] - top)
        acc = top + jnp.log(tot)
    o_ref[...] = acc


def combine(x, axis, n, mode, cid):
    size = x.shape[0]
    rows = size // 128
    x2 = x.reshape(rows, 128)
    out = pl.pallas_call(
        functools.partial(_combine_kernel, axis, n, mode),
        out_shape=jax.ShapeDtypeStruct((rows, 128), jnp.float32),
        in_specs=[pl.BlockSpec(memory_space=pltpu.VMEM)],
        out_specs=pl.BlockSpec(memory_space=pltpu.VMEM),
        scratch_shapes=[
            pltpu.VMEM((n, rows, 128), jnp.float32),
            pltpu.SemaphoreType.DMA((n,)),
            pltpu.SemaphoreType.DMA((n,)),
        ],
        compiler_params=pltpu.CompilerParams(collective_id=cid, has_side_effects=True),
    )(x2)
    return out.reshape(size)

from jax.sharding import PartitionSpec as P

ITERS = 3


SMOOTHING = 0.25


def _scatter_kernel(axis, n, x_ref, o_ref, buf, send_sem, recv_sem):
    me = lax.axis_index(axis)
    barrier = pltpu.get_barrier_semaphore()
    for k in range(1, n):
        pl.semaphore_signal(barrier, inc=1, device_id=_peer(axis, k, n), device_id_type=MESH)
    pl.semaphore_wait(barrier, n - 1)
    copies = []
    for k in range(1, n):
        copy = pltpu.make_async_remote_copy(
            src_ref=x_ref.at[lax.rem(me + k, n)],
            dst_ref=buf.at[k],
            send_sem=send_sem.at[k],
            recv_sem=recv_sem.at[k],
            device_id=_peer(axis, k, n),
            device_id_type=MESH,
        )
        copy.start()
        copies.append(copy)
    for copy in copies:
        copy.wait()
    acc = x_ref[me]
    for k in range(1, n):
        acc = acc + buf[k]
    o_ref[...] = acc


def scatter_sum(x, axis, cid):
    n = lax.axis_size(axis)
    rows = x.shape[0] // n
    lanes = x.shape[1]
    return pl.pallas_call(
        functools.partial(_scatter_kernel, axis, n),
        out_shape=jax.ShapeDtypeStruct((rows, lanes), jnp.float32),
        in_specs=[pl.BlockSpec(memory_space=pltpu.VMEM)],
        out_specs=pl.BlockSpec(memory_space=pltpu.VMEM),
        scratch_shapes=[
            pltpu.VMEM((n, rows, lanes), jnp.float32),
            pltpu.SemaphoreType.DMA((n,)),
            pltpu.SemaphoreType.DMA((n,)),
        ],
        compiler_params=pltpu.CompilerParams(collective_id=cid, has_side_effects=True),
    )(x.reshape(n, rows, lanes))


_IDS = {("cap", "lse"): 0, ("img", "lse"): 1, ("cap", "sum"): 2, ("img", "sum"): 3}


def gathered_lse(part, axis):
    return combine(part, axis, lax.axis_size(axis), "lse", _IDS[(axis, "lse")])


def gathered_sum(part, axis):
    return combine(part, axis, lax.axis_size(axis), "sum", _IDS[(axis, "sum")])


TM = 1024
INV_EPS = 1.0 / SMOOTHING


def _scores_t(img_ref, cap_ref, inv_root):
    return lax.dot_general(
        cap_ref[...], img_ref[...], (((1,), (1,)), ((), ())), preferred_element_type=jnp.float32
    ) * inv_root


def _lane_chunks(x):
    return [x[:, k * 128:(k + 1) * 128] for k in range(x.shape[1] // 128)]


def _row_kernel(mode, inv_root, img_ref, cap_ref, a_ref, b_ref, w_ref, o_ref):
    s = _scores_t(img_ref, cap_ref, inv_root)
    if mode == "lse":
        x = (b_ref[...] + s) * INV_EPS
        top = jnp.max(x, axis=0, keepdims=True)
        o_ref[...] = top + jnp.log(jnp.sum(jnp.exp(x - top), axis=0, keepdims=True))
    else:
        plan = jnp.exp((a_ref[...] + s) * INV_EPS - b_ref[...])
        o_ref[...] = jnp.sum(plan * w_ref[...], axis=0, keepdims=True)


def _specs(n, c, e):
    return [
        pl.BlockSpec((TM, e), lambda i: (i, 0)),
        pl.BlockSpec((c, e), lambda i: (0, 0)),
        pl.BlockSpec((1, TM), lambda i: (0, i)),
        pl.BlockSpec((c, 1), lambda i: (0, 0)),
    ]


def row_pass(mode, images, captions, a, b, w):
    n, e = images.shape
    c = captions.shape[0]
    inv_root = 1.0 / math.sqrt(e)
    out = pl.pallas_call(
        functools.partial(_row_kernel, mode, inv_root),
        out_shape=jax.ShapeDtypeStruct((1, n), jnp.float32),
        grid=(n // TM,),
        in_specs=_specs(n, c, e) + [pl.BlockSpec((c, 1), lambda i: (0, 0))],
        out_specs=pl.BlockSpec((1, TM), lambda i: (0, i)),
        cost_estimate=pl.CostEstimate(
            flops=2 * n * c * e, transcendentals=n * c, bytes_accessed=n * e * 2 + c * e * 2
        ),
    )(images, captions, a.reshape(1, n), b.reshape(c, 1), w.reshape(c, 1))
    return out.reshape(n)


def _col_kernel(mode, inv_root, img_ref, cap_ref, a_ref, b_ref, w_ref, o_ref, top_ref, tot_ref):
    step = pl.program_id(0)
    s = _scores_t(img_ref, cap_ref, inv_root)
    if mode == "lse":
        chunks = _lane_chunks((a_ref[...] + s) * INV_EPS)

        @pl.when(step == 0)
        def _():
            top_ref[...] = jnp.full(top_ref.shape, -jnp.inf, jnp.float32)
            tot_ref[...] = jnp.zeros(tot_ref.shape, jnp.float32)

        cmax = chunks[0]
        for piece in chunks[1:]:
            cmax = jnp.maximum(cmax, piece)
        old = top_ref[...]
        top = jnp.maximum(old, cmax)
        tot = tot_ref[...] * jnp.exp(old - top)
        for piece in chunks:
            tot = tot + jnp.exp(piece - top)
        tot_ref[...] = tot
        top_ref[...] = top

        @pl.when(step == pl.num_programs(0) - 1)
        def _():
            t = top_ref[...]
            m = jnp.max(t, axis=1, keepdims=True)
            o_ref[...] = m + jnp.log(jnp.sum(tot_ref[...] * jnp.exp(t - m), axis=1, keepdims=True))
    else:
        plan = jnp.exp((b_ref[...] + s) * INV_EPS - a_ref[...])
        chunks = _lane_chunks(plan * w_ref[...])

        @pl.when(step == 0)
        def _():
            tot_ref[...] = jnp.zeros(tot_ref.shape, jnp.float32)

        acc = chunks[0]
        for piece in chunks[1:]:
            acc = acc + piece
        tot_ref[...] += acc

        @pl.when(step == pl.num_programs(0) - 1)
        def _():
            o_ref[...] = jnp.sum(tot_ref[...], axis=1, keepdims=True)


def col_pass(mode, images, captions, a, w, b):
    n, e = images.shape
    c = captions.shape[0]
    inv_root = 1.0 / math.sqrt(e)
    out = pl.pallas_call(
        functools.partial(_col_kernel, mode, inv_root),
        out_shape=jax.ShapeDtypeStruct((c, 1), jnp.float32),
        grid=(n // TM,),
        in_specs=_specs(n, c, e) + [pl.BlockSpec((1, TM), lambda i: (0, i))],
        out_specs=pl.BlockSpec((c, 1), lambda i: (0, 0)),
        scratch_shapes=[pltpu.VMEM((c, 128), jnp.float32), pltpu.VMEM((c, 128), jnp.float32)],
        cost_estimate=pl.CostEstimate(
            flops=2 * n * c * e, transcendentals=n * c, bytes_accessed=n * e * 2 + c * e * 2
        ),
    )(images, captions, a.reshape(1, n), b.reshape(c, 1), w.reshape(1, n))
    return out.reshape(c)


def _final_kernel(inv_root, img_ref, cap_ref, rows_ref, cols_ref, ig_ref, cg_ref):
    step = pl.program_id(0)
    s = _scores_t(img_ref, cap_ref, inv_root)
    rows = rows_ref[...]
    cols = cols_ref[...]
    logw_r = rows[6:7, :]
    logw_c = cols[:, 7:8]
    adjoint = jnp.zeros(s.shape, jnp.float32)
    for level in reversed(range(ITERS)):
        f = rows[level:level + 1, :]
        fb = rows[3 + level:4 + level, :]
        g_prev = cols[:, level:level + 1]
        g = cols[:, level + 1:level + 2]
        gb = cols[:, 4 + level:5 + level]
        col_plan = jnp.exp((f + s) * INV_EPS - (logw_c - g * INV_EPS))
        adjoint = adjoint - col_plan * gb
        row_plan = jnp.exp((g_prev + s) * INV_EPS - (logw_r - f * INV_EPS))
        adjoint = adjoint - row_plan * fb
    rounded = adjoint.astype(jnp.bfloat16)
    ig_ref[...] = lax.dot_general(
        rounded, cap_ref[...], (((0,), (0,)), ((), ())), preferred_element_type=jnp.float32
    ) * inv_root

    @pl.when(step == 0)
    def _():
        cg_ref[...] = jnp.zeros(cg_ref.shape, jnp.float32)

    cg_ref[...] += jnp.dot(rounded, img_ref[...], preferred_element_type=jnp.float32) * inv_root


def final_pass(images, captions, rows, cols):
    n, e = images.shape
    c = captions.shape[0]
    inv_root = 1.0 / math.sqrt(e)
    return pl.pallas_call(
        functools.partial(_final_kernel, inv_root),
        out_shape=(
            jax.ShapeDtypeStruct((n, e), jnp.float32),
            jax.ShapeDtypeStruct((c, e), jnp.float32),
        ),
        grid=(n // TM,),
        in_specs=[
            pl.BlockSpec((TM, e), lambda i: (i, 0)),
            pl.BlockSpec((c, e), lambda i: (0, 0)),
            pl.BlockSpec((8, TM), lambda i: (0, i)),
            pl.BlockSpec((c, 8), lambda i: (0, 0)),
        ],
        out_specs=(
            pl.BlockSpec((TM, e), lambda i: (i, 0)),
            pl.BlockSpec((c, e), lambda i: (0, 0)),
        ),
        cost_estimate=pl.CostEstimate(
            flops=6 * n * c * e, transcendentals=6 * n * c, bytes_accessed=n * e * 6 + c * e * 6
        ),
    )(images, captions, rows, cols)


def body(images, captions, image_logw, caption_logw, image_cot, caption_cot):
    n = images.shape[0]
    c = captions.shape[0]
    zeros_r = jnp.zeros((n,), jnp.float32)
    zeros_c = jnp.zeros((c,), jnp.float32)
    col_hist = [zeros_c]
    row_hist = []
    for level in range(ITERS):
        part = row_pass("lse", images, captions, zeros_r, col_hist[-1], zeros_c)
        row_pot = SMOOTHING * image_logw - SMOOTHING * gathered_lse(part, "cap")
        row_hist.append(row_pot)
        part = col_pass("lse", images, captions, row_pot, zeros_r, zeros_c)
        col_hist.append(SMOOTHING * caption_logw - SMOOTHING * gathered_lse(part, "img"))
    col_bar = caption_cot
    row_bars = [None] * ITERS
    col_bars = [None] * ITERS
    for level in reversed(range(ITERS)):
        col_bars[level] = col_bar
        shift_col = caption_logw - col_hist[level + 1] / SMOOTHING
        part = row_pass("wsum", images, captions, row_hist[level], shift_col, col_bar)
        row_bar = -gathered_sum(part, "cap")
        if level == ITERS - 1:
            row_bar = image_cot + row_bar
        row_bars[level] = row_bar
        if level > 0:
            shift_row = image_logw - row_hist[level] / SMOOTHING
            part = col_pass("wsum", images, captions, shift_row, row_bar, col_hist[level])
            col_bar = -gathered_sum(part, "img")
    rows = jnp.stack(row_hist + row_bars + [image_logw, zeros_r], axis=0)
    cols = jnp.stack(col_hist + col_bars + [caption_logw], axis=1)
    ig_part, cg_part = final_pass(images, captions, rows, cols)
    image_grad = lax.psum_scatter(ig_part, "cap", scatter_dimension=0, tiled=True)
    caption_grad = scatter_sum(cg_part, "img", 4)
    return (image_grad, caption_grad)


def solution(mesh):
    in_specs = (P("img", None), P("cap", None), P("img"), P("cap"), P("img"), P("cap"))
    out_specs = (P(("img", "cap"), None), P(("cap", "img"), None))
    return jax.shard_map(body, mesh=mesh, in_specs=in_specs, out_specs=out_specs, check_vma=False)
```

```python
import functools
import math

import jax
import jax.numpy as jnp
from jax import lax
from jax.experimental import pallas as pl
from jax.experimental.pallas import tpu as pltpu

MESH = pl.DeviceIdType.MESH


def _peer(axis, k, n):
    me_img = lax.axis_index("img")
    me_cap = lax.axis_index("cap")
    if axis == "cap":
        return (me_img, lax.rem(me_cap + k, n))
    return (lax.rem(me_img + k, n), me_cap)


def _combine_kernel(axis, n, mode, x_ref, o_ref, buf, send_sem, recv_sem):
    barrier = pltpu.get_barrier_semaphore()
    for k in range(1, n):
        pl.semaphore_signal(barrier, inc=1, device_id=_peer(axis, k, n), device_id_type=MESH)
    pl.semaphore_wait(barrier, n - 1)
    copies = []
    for k in range(1, n):
        copy = pltpu.make_async_remote_copy(
            src_ref=x_ref,
            dst_ref=buf.at[k],
            send_sem=send_sem.at[k],
            recv_sem=recv_sem.at[k],
            device_id=_peer(axis, k, n),
            device_id_type=MESH,
        )
        copy.start()
        copies.append(copy)
    for copy in copies:
        copy.wait()
    x = x_ref[...]
    if mode == "sum":
        acc = x
        for k in range(1, n):
            acc = acc + buf[k]
    else:
        top = x
        for k in range(1, n):
            top = jnp.maximum(top, buf[k])
        tot = jnp.exp(x - top)
        for k in range(1, n):
            tot = tot + jnp.exp(buf[k] - top)
        acc = top + jnp.log(tot)
    o_ref[...] = acc


def combine(x, axis, n, mode, cid):
    size = x.shape[0]
    rows = size // 128
    x2 = x.reshape(rows, 128)
    out = pl.pallas_call(
        functools.partial(_combine_kernel, axis, n, mode),
        out_shape=jax.ShapeDtypeStruct((rows, 128), jnp.float32),
        in_specs=[pl.BlockSpec(memory_space=pltpu.VMEM)],
        out_specs=pl.BlockSpec(memory_space=pltpu.VMEM),
        scratch_shapes=[
            pltpu.VMEM((n, rows, 128), jnp.float32),
            pltpu.SemaphoreType.DMA((n,)),
            pltpu.SemaphoreType.DMA((n,)),
        ],
        compiler_params=pltpu.CompilerParams(collective_id=cid, has_side_effects=True),
    )(x2)
    return out.reshape(size)

from jax.sharding import PartitionSpec as P

ITERS = 3


SMOOTHING = 0.25


def _scatter_kernel(axis, n, x_ref, o_ref, buf, send_sem, recv_sem):
    me = lax.axis_index(axis)
    barrier = pltpu.get_barrier_semaphore()
    for k in range(1, n):
        pl.semaphore_signal(barrier, inc=1, device_id=_peer(axis, k, n), device_id_type=MESH)
    pl.semaphore_wait(barrier, n - 1)
    copies = []
    for k in range(1, n):
        copy = pltpu.make_async_remote_copy(
            src_ref=x_ref.at[lax.rem(me + k, n)],
            dst_ref=buf.at[k],
            send_sem=send_sem.at[k],
            recv_sem=recv_sem.at[k],
            device_id=_peer(axis, k, n),
            device_id_type=MESH,
        )
        copy.start()
        copies.append(copy)
    for copy in copies:
        copy.wait()
    acc = x_ref[me]
    for k in range(1, n):
        acc = acc + buf[k]
    o_ref[...] = acc


def scatter_sum(x, axis, cid):
    n = lax.axis_size(axis)
    rows = x.shape[0] // n
    lanes = x.shape[1]
    return pl.pallas_call(
        functools.partial(_scatter_kernel, axis, n),
        out_shape=jax.ShapeDtypeStruct((rows, lanes), jnp.float32),
        in_specs=[pl.BlockSpec(memory_space=pltpu.VMEM)],
        out_specs=pl.BlockSpec(memory_space=pltpu.VMEM),
        scratch_shapes=[
            pltpu.VMEM((n, rows, lanes), jnp.float32),
            pltpu.SemaphoreType.DMA((n,)),
            pltpu.SemaphoreType.DMA((n,)),
        ],
        compiler_params=pltpu.CompilerParams(collective_id=cid, has_side_effects=True),
    )(x.reshape(n, rows, lanes))


_IDS = {("cap", "lse"): 0, ("img", "lse"): 1, ("cap", "sum"): 2, ("img", "sum"): 3}


def gathered_lse(part, axis):
    return combine(part, axis, lax.axis_size(axis), "lse", _IDS[(axis, "lse")])


def gathered_sum(part, axis):
    return combine(part, axis, lax.axis_size(axis), "sum", _IDS[(axis, "sum")])


TM = 1024
INV_EPS = 1.0 / SMOOTHING


def _scores_t(img_ref, cap_ref, inv_root):
    return lax.dot_general(
        cap_ref[...], img_ref[...], (((1,), (1,)), ((), ())), preferred_element_type=jnp.float32
    ) * inv_root


def _lane_chunks(x):
    return [x[:, k * 128:(k + 1) * 128] for k in range(x.shape[1] // 128)]


def _row_kernel(mode, inv_root, img_ref, cap_ref, a_ref, b_ref, w_ref, o_ref):
    s = _scores_t(img_ref, cap_ref, inv_root)
    if mode == "lse":
        x = (b_ref[...] + s) * INV_EPS
        top = jnp.max(x, axis=0, keepdims=True)
        o_ref[...] = top + jnp.log(jnp.sum(jnp.exp(x - top), axis=0, keepdims=True))
    else:
        plan = jnp.exp((a_ref[...] + s) * INV_EPS - b_ref[...])
        o_ref[...] = jnp.sum(plan * w_ref[...], axis=0, keepdims=True)


def _specs(n, c, e):
    return [
        pl.BlockSpec((TM, e), lambda i: (i, 0)),
        pl.BlockSpec((c, e), lambda i: (0, 0)),
        pl.BlockSpec((1, TM), lambda i: (0, i)),
        pl.BlockSpec((c, 1), lambda i: (0, 0)),
    ]


def row_pass(mode, images, captions, a, b, w):
    n, e = images.shape
    c = captions.shape[0]
    inv_root = 1.0 / math.sqrt(e)
    out = pl.pallas_call(
        functools.partial(_row_kernel, mode, inv_root),
        out_shape=jax.ShapeDtypeStruct((1, n), jnp.float32),
        grid=(n // TM,),
        in_specs=_specs(n, c, e) + [pl.BlockSpec((c, 1), lambda i: (0, 0))],
        out_specs=pl.BlockSpec((1, TM), lambda i: (0, i)),
        cost_estimate=pl.CostEstimate(
            flops=2 * n * c * e, transcendentals=n * c, bytes_accessed=n * e * 2 + c * e * 2
        ),
    )(images, captions, a.reshape(1, n), b.reshape(c, 1), w.reshape(c, 1))
    return out.reshape(n)


def _col_kernel(mode, inv_root, img_ref, cap_ref, a_ref, b_ref, w_ref, o_ref, top_ref, tot_ref):
    step = pl.program_id(0)
    s = _scores_t(img_ref, cap_ref, inv_root)
    if mode == "lse":
        chunks = _lane_chunks((a_ref[...] + s) * INV_EPS)

        @pl.when(step == 0)
        def _():
            top_ref[...] = jnp.full(top_ref.shape, -jnp.inf, jnp.float32)
            tot_ref[...] = jnp.zeros(tot_ref.shape, jnp.float32)

        cmax = chunks[0]
        for piece in chunks[1:]:
            cmax = jnp.maximum(cmax, piece)
        old = top_ref[...]
        top = jnp.maximum(old, cmax)
        tot = tot_ref[...] * jnp.exp(old - top)
        for piece in chunks:
            tot = tot + jnp.exp(piece - top)
        tot_ref[...] = tot
        top_ref[...] = top

        @pl.when(step == pl.num_programs(0) - 1)
        def _():
            t = top_ref[...]
            m = jnp.max(t, axis=1, keepdims=True)
            o_ref[...] = m + jnp.log(jnp.sum(tot_ref[...] * jnp.exp(t - m), axis=1, keepdims=True))
    else:
        plan = jnp.exp((b_ref[...] + s) * INV_EPS - a_ref[...])
        chunks = _lane_chunks(plan * w_ref[...])

        @pl.when(step == 0)
        def _():
            tot_ref[...] = jnp.zeros(tot_ref.shape, jnp.float32)

        acc = chunks[0]
        for piece in chunks[1:]:
            acc = acc + piece
        tot_ref[...] += acc

        @pl.when(step == pl.num_programs(0) - 1)
        def _():
            o_ref[...] = jnp.sum(tot_ref[...], axis=1, keepdims=True)


def col_pass(mode, images, captions, a, w, b):
    n, e = images.shape
    c = captions.shape[0]
    inv_root = 1.0 / math.sqrt(e)
    out = pl.pallas_call(
        functools.partial(_col_kernel, mode, inv_root),
        out_shape=jax.ShapeDtypeStruct((c, 1), jnp.float32),
        grid=(n // TM,),
        in_specs=_specs(n, c, e) + [pl.BlockSpec((1, TM), lambda i: (0, i))],
        out_specs=pl.BlockSpec((c, 1), lambda i: (0, 0)),
        scratch_shapes=[pltpu.VMEM((c, 128), jnp.float32), pltpu.VMEM((c, 128), jnp.float32)],
        cost_estimate=pl.CostEstimate(
            flops=2 * n * c * e, transcendentals=n * c, bytes_accessed=n * e * 2 + c * e * 2
        ),
    )(images, captions, a.reshape(1, n), b.reshape(c, 1), w.reshape(1, n))
    return out.reshape(c)


def _final_kernel(inv_root, img_ref, cap_ref, rows_ref, cols_ref, ia_ref, ib_ref, cg_ref):
    step = pl.program_id(0)
    s = _scores_t(img_ref, cap_ref, inv_root)
    rows = rows_ref[...]
    cols = cols_ref[...]
    logw_r = rows[6:7, :]
    logw_c = cols[:, 7:8]
    adjoint = jnp.zeros(s.shape, jnp.float32)
    for level in reversed(range(ITERS)):
        f = rows[level:level + 1, :]
        fb = rows[3 + level:4 + level, :]
        g_prev = cols[:, level:level + 1]
        g = cols[:, level + 1:level + 2]
        gb = cols[:, 4 + level:5 + level]
        col_plan = jnp.exp((f + s) * INV_EPS - (logw_c - g * INV_EPS))
        adjoint = adjoint - col_plan * gb
        row_plan = jnp.exp((g_prev + s) * INV_EPS - (logw_r - f * INV_EPS))
        adjoint = adjoint - row_plan * fb
    rounded = adjoint.astype(jnp.bfloat16)
    ig = lax.dot_general(
        rounded, cap_ref[...], (((0,), (0,)), ((), ())), preferred_element_type=jnp.float32
    ) * inv_root
    ig = ig.reshape(ia_ref.shape[0], 2, ia_ref.shape[1], ia_ref.shape[2])
    ia_ref[...] = ig[:, 0]
    ib_ref[...] = ig[:, 1]

    @pl.when(step == 0)
    def _():
        cg_ref[...] = jnp.zeros(cg_ref.shape, jnp.float32)

    cg_ref[...] += jnp.dot(rounded, img_ref[...], preferred_element_type=jnp.float32) * inv_root


def final_pass(images, captions, rows, cols, owners):
    n, e = images.shape
    c = captions.shape[0]
    inv_root = 1.0 / math.sqrt(e)
    half = n // owners // 2
    per_tile = TM // (2 * half)
    return pl.pallas_call(
        functools.partial(_final_kernel, inv_root),
        out_shape=(
            jax.ShapeDtypeStruct((owners, half, e), jnp.float32),
            jax.ShapeDtypeStruct((owners, half, e), jnp.float32),
            jax.ShapeDtypeStruct((c, e), jnp.float32),
        ),
        grid=(n // TM,),
        in_specs=[
            pl.BlockSpec((TM, e), lambda i: (i, 0)),
            pl.BlockSpec((c, e), lambda i: (0, 0)),
            pl.BlockSpec((8, TM), lambda i: (0, i)),
            pl.BlockSpec((c, 8), lambda i: (0, 0)),
        ],
        out_specs=(
            pl.BlockSpec((per_tile, half, e), lambda i: (i, 0, 0)),
            pl.BlockSpec((per_tile, half, e), lambda i: (i, 0, 0)),
            pl.BlockSpec((c, e), lambda i: (0, 0)),
        ),
        cost_estimate=pl.CostEstimate(
            flops=6 * n * c * e, transcendentals=6 * n * c, bytes_accessed=n * e * 6 + c * e * 6
        ),
    )(images, captions, rows, cols)


def body(images, captions, image_logw, caption_logw, image_cot, caption_cot):
    n = images.shape[0]
    c = captions.shape[0]
    zeros_r = jnp.zeros((n,), jnp.float32)
    zeros_c = jnp.zeros((c,), jnp.float32)
    col_hist = [zeros_c]
    row_hist = []
    for level in range(ITERS):
        part = row_pass("lse", images, captions, zeros_r, col_hist[-1], zeros_c)
        row_pot = SMOOTHING * image_logw - SMOOTHING * gathered_lse(part, "cap")
        row_hist.append(row_pot)
        part = col_pass("lse", images, captions, row_pot, zeros_r, zeros_c)
        col_hist.append(SMOOTHING * caption_logw - SMOOTHING * gathered_lse(part, "img"))
    col_bar = caption_cot
    row_bars = [None] * ITERS
    col_bars = [None] * ITERS
    for level in reversed(range(ITERS)):
        col_bars[level] = col_bar
        shift_col = caption_logw - col_hist[level + 1] / SMOOTHING
        part = row_pass("wsum", images, captions, row_hist[level], shift_col, col_bar)
        row_bar = -gathered_sum(part, "cap")
        if level == ITERS - 1:
            row_bar = image_cot + row_bar
        row_bars[level] = row_bar
        if level > 0:
            shift_row = image_logw - row_hist[level] / SMOOTHING
            part = col_pass("wsum", images, captions, shift_row, row_bar, col_hist[level])
            col_bar = -gathered_sum(part, "img")
    rows = jnp.stack(row_hist + row_bars + [image_logw, zeros_r], axis=0)
    cols = jnp.stack(col_hist + col_bars + [caption_logw], axis=1)
    owners = lax.axis_size("cap")
    ig_a, ig_b, cg_part = final_pass(images, captions, rows, cols, owners)
    got_a = lax.psum_scatter(ig_a.reshape(-1, ig_a.shape[2]), "cap", scatter_dimension=0, tiled=True)
    got_b = scatter_sum(ig_b.reshape(-1, ig_b.shape[2]), "cap", 5)
    image_grad = jnp.concatenate([got_a, got_b], axis=0)
    caption_grad = scatter_sum(cg_part, "img", 4)
    return (image_grad, caption_grad)


def solution(mesh):
    in_specs = (P("img", None), P("cap", None), P("img"), P("cap"), P("img"), P("cap"))
    out_specs = (P(("img", "cap"), None), P(("cap", "img"), None))
    return jax.shard_map(body, mesh=mesh, in_specs=in_specs, out_specs=out_specs, check_vma=False)
```

```python
import functools
import math

import jax
import jax.numpy as jnp
from jax import lax
from jax.experimental import pallas as pl
from jax.experimental.pallas import tpu as pltpu

MESH = pl.DeviceIdType.MESH


def _peer(axis, k, n):
    me_img = lax.axis_index("img")
    me_cap = lax.axis_index("cap")
    if axis == "cap":
        return (me_img, lax.rem(me_cap + k, n))
    return (lax.rem(me_img + k, n), me_cap)


def _combine_kernel(axis, n, mode, x_ref, o_ref, buf, send_sem, recv_sem):
    barrier = pltpu.get_barrier_semaphore()
    for k in range(1, n):
        pl.semaphore_signal(barrier, inc=1, device_id=_peer(axis, k, n), device_id_type=MESH)
    pl.semaphore_wait(barrier, n - 1)
    copies = []
    for k in range(1, n):
        copy = pltpu.make_async_remote_copy(
            src_ref=x_ref,
            dst_ref=buf.at[k],
            send_sem=send_sem.at[k],
            recv_sem=recv_sem.at[k],
            device_id=_peer(axis, k, n),
            device_id_type=MESH,
        )
        copy.start()
        copies.append(copy)
    for copy in copies:
        copy.wait()
    x = x_ref[...]
    if mode == "sum":
        acc = x
        for k in range(1, n):
            acc = acc + buf[k]
    else:
        top = x
        for k in range(1, n):
            top = jnp.maximum(top, buf[k])
        tot = jnp.exp(x - top)
        for k in range(1, n):
            tot = tot + jnp.exp(buf[k] - top)
        acc = top + jnp.log(tot)
    o_ref[...] = acc


def combine(x, axis, n, mode, cid):
    size = x.shape[0]
    rows = size // 128
    x2 = x.reshape(rows, 128)
    out = pl.pallas_call(
        functools.partial(_combine_kernel, axis, n, mode),
        out_shape=jax.ShapeDtypeStruct((rows, 128), jnp.float32),
        in_specs=[pl.BlockSpec(memory_space=pltpu.VMEM)],
        out_specs=pl.BlockSpec(memory_space=pltpu.VMEM),
        scratch_shapes=[
            pltpu.VMEM((n, rows, 128), jnp.float32),
            pltpu.SemaphoreType.DMA((n,)),
            pltpu.SemaphoreType.DMA((n,)),
        ],
        compiler_params=pltpu.CompilerParams(collective_id=cid, has_side_effects=True),
    )(x2)
    return out.reshape(size)

from jax.sharding import PartitionSpec as P

ITERS = 3


SMOOTHING = 0.25


def _scatter_kernel(axis, n, x_ref, o_ref, buf, send_sem, recv_sem):
    me = lax.axis_index(axis)
    barrier = pltpu.get_barrier_semaphore()
    for k in range(1, n):
        pl.semaphore_signal(barrier, inc=1, device_id=_peer(axis, k, n), device_id_type=MESH)
    pl.semaphore_wait(barrier, n - 1)
    copies = []
    for k in range(1, n):
        copy = pltpu.make_async_remote_copy(
            src_ref=x_ref.at[lax.rem(me + k, n)],
            dst_ref=buf.at[k],
            send_sem=send_sem.at[k],
            recv_sem=recv_sem.at[k],
            device_id=_peer(axis, k, n),
            device_id_type=MESH,
        )
        copy.start()
        copies.append(copy)
    for copy in copies:
        copy.wait()
    acc = x_ref[me]
    for k in range(1, n):
        acc = acc + buf[k]
    o_ref[...] = acc


def scatter_sum(x, axis, cid):
    n = lax.axis_size(axis)
    rows = x.shape[0] // n
    lanes = x.shape[1]
    return pl.pallas_call(
        functools.partial(_scatter_kernel, axis, n),
        out_shape=jax.ShapeDtypeStruct((rows, lanes), jnp.float32),
        in_specs=[pl.BlockSpec(memory_space=pltpu.VMEM)],
        out_specs=pl.BlockSpec(memory_space=pltpu.VMEM),
        scratch_shapes=[
            pltpu.VMEM((n, rows, lanes), jnp.float32),
            pltpu.SemaphoreType.DMA((n,)),
            pltpu.SemaphoreType.DMA((n,)),
        ],
        compiler_params=pltpu.CompilerParams(collective_id=cid, has_side_effects=True),
    )(x.reshape(n, rows, lanes))


_IDS = {("cap", "lse"): 0, ("img", "lse"): 1, ("cap", "sum"): 2, ("img", "sum"): 3}


def gathered_lse(part, axis):
    return combine(part, axis, lax.axis_size(axis), "lse", _IDS[(axis, "lse")])


def gathered_sum(part, axis):
    return combine(part, axis, lax.axis_size(axis), "sum", _IDS[(axis, "sum")])


TM = 1024
TM_PASS = 2048
INV_EPS = 1.0 / SMOOTHING


def _scores_t(img_ref, cap_ref, inv_root):
    return lax.dot_general(
        cap_ref[...], img_ref[...], (((1,), (1,)), ((), ())), preferred_element_type=jnp.float32
    ) * inv_root


def _lane_chunks(x):
    return [x[:, k * 128:(k + 1) * 128] for k in range(x.shape[1] // 128)]


def _row_kernel(mode, inv_root, img_ref, cap_ref, a_ref, b_ref, w_ref, o_ref):
    s = _scores_t(img_ref, cap_ref, inv_root)
    if mode == "lse":
        x = (b_ref[...] + s) * INV_EPS
        top = jnp.max(x, axis=0, keepdims=True)
        o_ref[...] = top + jnp.log(jnp.sum(jnp.exp(x - top), axis=0, keepdims=True))
    else:
        plan = jnp.exp((a_ref[...] + s) * INV_EPS - b_ref[...])
        o_ref[...] = jnp.sum(plan * w_ref[...], axis=0, keepdims=True)


def _specs(n, c, e):
    return [
        pl.BlockSpec((TM_PASS, e), lambda i: (i, 0)),
        pl.BlockSpec((c, e), lambda i: (0, 0)),
        pl.BlockSpec((1, TM_PASS), lambda i: (0, i)),
        pl.BlockSpec((c, 1), lambda i: (0, 0)),
    ]


def row_pass(mode, images, captions, a, b, w):
    n, e = images.shape
    c = captions.shape[0]
    inv_root = 1.0 / math.sqrt(e)
    out = pl.pallas_call(
        functools.partial(_row_kernel, mode, inv_root),
        out_shape=jax.ShapeDtypeStruct((1, n), jnp.float32),
        grid=(n // TM_PASS,),
        in_specs=_specs(n, c, e) + [pl.BlockSpec((c, 1), lambda i: (0, 0))],
        out_specs=pl.BlockSpec((1, TM_PASS), lambda i: (0, i)),
        cost_estimate=pl.CostEstimate(
            flops=2 * n * c * e, transcendentals=n * c, bytes_accessed=n * e * 2 + c * e * 2
        ),
    )(images, captions, a.reshape(1, n), b.reshape(c, 1), w.reshape(c, 1))
    return out.reshape(n)


def _col_kernel(mode, inv_root, img_ref, cap_ref, a_ref, b_ref, w_ref, o_ref, top_ref, tot_ref):
    step = pl.program_id(0)
    s = _scores_t(img_ref, cap_ref, inv_root)
    if mode == "lse":
        chunks = _lane_chunks((a_ref[...] + s) * INV_EPS)

        @pl.when(step == 0)
        def _():
            top_ref[...] = jnp.full(top_ref.shape, -jnp.inf, jnp.float32)
            tot_ref[...] = jnp.zeros(tot_ref.shape, jnp.float32)

        cmax = chunks[0]
        for piece in chunks[1:]:
            cmax = jnp.maximum(cmax, piece)
        old = top_ref[...]
        top = jnp.maximum(old, cmax)
        tot = tot_ref[...] * jnp.exp(old - top)
        for piece in chunks:
            tot = tot + jnp.exp(piece - top)
        tot_ref[...] = tot
        top_ref[...] = top

        @pl.when(step == pl.num_programs(0) - 1)
        def _():
            t = top_ref[...]
            m = jnp.max(t, axis=1, keepdims=True)
            o_ref[...] = m + jnp.log(jnp.sum(tot_ref[...] * jnp.exp(t - m), axis=1, keepdims=True))
    else:
        plan = jnp.exp((b_ref[...] + s) * INV_EPS - a_ref[...])
        chunks = _lane_chunks(plan * w_ref[...])

        @pl.when(step == 0)
        def _():
            tot_ref[...] = jnp.zeros(tot_ref.shape, jnp.float32)

        acc = chunks[0]
        for piece in chunks[1:]:
            acc = acc + piece
        tot_ref[...] += acc

        @pl.when(step == pl.num_programs(0) - 1)
        def _():
            o_ref[...] = jnp.sum(tot_ref[...], axis=1, keepdims=True)


def col_pass(mode, images, captions, a, w, b):
    n, e = images.shape
    c = captions.shape[0]
    inv_root = 1.0 / math.sqrt(e)
    out = pl.pallas_call(
        functools.partial(_col_kernel, mode, inv_root),
        out_shape=jax.ShapeDtypeStruct((c, 1), jnp.float32),
        grid=(n // TM_PASS,),
        in_specs=_specs(n, c, e) + [pl.BlockSpec((1, TM_PASS), lambda i: (0, i))],
        out_specs=pl.BlockSpec((c, 1), lambda i: (0, 0)),
        scratch_shapes=[pltpu.VMEM((c, 128), jnp.float32), pltpu.VMEM((c, 128), jnp.float32)],
        cost_estimate=pl.CostEstimate(
            flops=2 * n * c * e, transcendentals=n * c, bytes_accessed=n * e * 2 + c * e * 2
        ),
    )(images, captions, a.reshape(1, n), b.reshape(c, 1), w.reshape(1, n))
    return out.reshape(c)


def _final_kernel(inv_root, img_ref, cap_ref, rows_ref, cols_ref, ig_ref, cg_ref):
    step = pl.program_id(0)
    s = _scores_t(img_ref, cap_ref, inv_root)
    rows = rows_ref[...]
    cols = cols_ref[...]
    logw_r = rows[6:7, :]
    logw_c = cols[:, 7:8]
    adjoint = jnp.zeros(s.shape, jnp.float32)
    for level in reversed(range(ITERS)):
        f = rows[level:level + 1, :]
        fb = rows[3 + level:4 + level, :]
        g_prev = cols[:, level:level + 1]
        g = cols[:, level + 1:level + 2]
        gb = cols[:, 4 + level:5 + level]
        col_plan = jnp.exp((f + s) * INV_EPS - (logw_c - g * INV_EPS))
        adjoint = adjoint - col_plan * gb
        row_plan = jnp.exp((g_prev + s) * INV_EPS - (logw_r - f * INV_EPS))
        adjoint = adjoint - row_plan * fb
    rounded = adjoint.astype(jnp.bfloat16)
    ig_ref[...] = lax.dot_general(
        rounded, cap_ref[...], (((0,), (0,)), ((), ())), preferred_element_type=jnp.float32
    ) * inv_root

    @pl.when(step == 0)
    def _():
        cg_ref[...] = jnp.zeros(cg_ref.shape, jnp.float32)

    cg_ref[...] += jnp.dot(rounded, img_ref[...], preferred_element_type=jnp.float32) * inv_root


def final_pass(images, captions, rows, cols):
    n, e = images.shape
    c = captions.shape[0]
    inv_root = 1.0 / math.sqrt(e)
    return pl.pallas_call(
        functools.partial(_final_kernel, inv_root),
        out_shape=(
            jax.ShapeDtypeStruct((n, e), jnp.float32),
            jax.ShapeDtypeStruct((c, e), jnp.float32),
        ),
        grid=(n // TM,),
        in_specs=[
            pl.BlockSpec((TM, e), lambda i: (i, 0)),
            pl.BlockSpec((c, e), lambda i: (0, 0)),
            pl.BlockSpec((8, TM), lambda i: (0, i)),
            pl.BlockSpec((c, 8), lambda i: (0, 0)),
        ],
        out_specs=(
            pl.BlockSpec((TM, e), lambda i: (i, 0)),
            pl.BlockSpec((c, e), lambda i: (0, 0)),
        ),
        cost_estimate=pl.CostEstimate(
            flops=6 * n * c * e, transcendentals=6 * n * c, bytes_accessed=n * e * 6 + c * e * 6
        ),
    )(images, captions, rows, cols)


def body(images, captions, image_logw, caption_logw, image_cot, caption_cot):
    n = images.shape[0]
    c = captions.shape[0]
    zeros_r = jnp.zeros((n,), jnp.float32)
    zeros_c = jnp.zeros((c,), jnp.float32)
    col_hist = [zeros_c]
    row_hist = []
    for level in range(ITERS):
        part = row_pass("lse", images, captions, zeros_r, col_hist[-1], zeros_c)
        row_pot = SMOOTHING * image_logw - SMOOTHING * gathered_lse(part, "cap")
        row_hist.append(row_pot)
        part = col_pass("lse", images, captions, row_pot, zeros_r, zeros_c)
        col_hist.append(SMOOTHING * caption_logw - SMOOTHING * gathered_lse(part, "img"))
    col_bar = caption_cot
    row_bars = [None] * ITERS
    col_bars = [None] * ITERS
    for level in reversed(range(ITERS)):
        col_bars[level] = col_bar
        shift_col = caption_logw - col_hist[level + 1] / SMOOTHING
        part = row_pass("wsum", images, captions, row_hist[level], shift_col, col_bar)
        row_bar = -gathered_sum(part, "cap")
        if level == ITERS - 1:
            row_bar = image_cot + row_bar
        row_bars[level] = row_bar
        if level > 0:
            shift_row = image_logw - row_hist[level] / SMOOTHING
            part = col_pass("wsum", images, captions, shift_row, row_bar, col_hist[level])
            col_bar = -gathered_sum(part, "img")
    rows = jnp.stack(row_hist + row_bars + [image_logw, zeros_r], axis=0)
    cols = jnp.stack(col_hist + col_bars + [caption_logw], axis=1)
    ig_part, cg_part = final_pass(images, captions, rows, cols)
    image_grad = lax.psum_scatter(ig_part, "cap", scatter_dimension=0, tiled=True)
    caption_grad = scatter_sum(cg_part, "img", 4)
    return (image_grad, caption_grad)


def solution(mesh):
    in_specs = (P("img", None), P("cap", None), P("img"), P("cap"), P("img"), P("cap"))
    out_specs = (P(("img", "cap"), None), P(("cap", "img"), None))
    return jax.shard_map(body, mesh=mesh, in_specs=in_specs, out_specs=out_specs, check_vma=False)
```

```python
import functools
import math

import jax
import jax.numpy as jnp
from jax import lax
from jax.experimental import pallas as pl
from jax.experimental.pallas import tpu as pltpu

MESH = pl.DeviceIdType.MESH


def _peer(axis, k, n):
    me_img = lax.axis_index("img")
    me_cap = lax.axis_index("cap")
    if axis == "cap":
        return (me_img, lax.rem(me_cap + k, n))
    return (lax.rem(me_img + k, n), me_cap)


def _combine_kernel(axis, n, mode, x_ref, o_ref, buf, send_sem, recv_sem):
    barrier = pltpu.get_barrier_semaphore()
    for k in range(1, n):
        pl.semaphore_signal(barrier, inc=1, device_id=_peer(axis, k, n), device_id_type=MESH)
    pl.semaphore_wait(barrier, n - 1)
    copies = []
    for k in range(1, n):
        copy = pltpu.make_async_remote_copy(
            src_ref=x_ref,
            dst_ref=buf.at[k],
            send_sem=send_sem.at[k],
            recv_sem=recv_sem.at[k],
            device_id=_peer(axis, k, n),
            device_id_type=MESH,
        )
        copy.start()
        copies.append(copy)
    for copy in copies:
        copy.wait()
    x = x_ref[...]
    if mode == "sum":
        acc = x
        for k in range(1, n):
            acc = acc + buf[k]
    else:
        top = x
        for k in range(1, n):
            top = jnp.maximum(top, buf[k])
        tot = jnp.exp(x - top)
        for k in range(1, n):
            tot = tot + jnp.exp(buf[k] - top)
        acc = top + jnp.log(tot)
    o_ref[...] = acc


def combine(x, axis, n, mode, cid):
    size = x.shape[0]
    rows = size // 128
    x2 = x.reshape(rows, 128)
    out = pl.pallas_call(
        functools.partial(_combine_kernel, axis, n, mode),
        out_shape=jax.ShapeDtypeStruct((rows, 128), jnp.float32),
        in_specs=[pl.BlockSpec(memory_space=pltpu.VMEM)],
        out_specs=pl.BlockSpec(memory_space=pltpu.VMEM),
        scratch_shapes=[
            pltpu.VMEM((n, rows, 128), jnp.float32),
            pltpu.SemaphoreType.DMA((n,)),
            pltpu.SemaphoreType.DMA((n,)),
        ],
        compiler_params=pltpu.CompilerParams(collective_id=cid, has_side_effects=True),
    )(x2)
    return out.reshape(size)

from jax.sharding import PartitionSpec as P

ITERS = 3


SMOOTHING = 0.25


def _scatter_kernel(axis, n, x_ref, o_ref, buf, send_sem, recv_sem):
    me = lax.axis_index(axis)
    barrier = pltpu.get_barrier_semaphore()
    for k in range(1, n):
        pl.semaphore_signal(barrier, inc=1, device_id=_peer(axis, k, n), device_id_type=MESH)
    pl.semaphore_wait(barrier, n - 1)
    copies = []
    for k in range(1, n):
        copy = pltpu.make_async_remote_copy(
            src_ref=x_ref.at[lax.rem(me + k, n)],
            dst_ref=buf.at[k],
            send_sem=send_sem.at[k],
            recv_sem=recv_sem.at[k],
            device_id=_peer(axis, k, n),
            device_id_type=MESH,
        )
        copy.start()
        copies.append(copy)
    for copy in copies:
        copy.wait()
    acc = x_ref[me]
    for k in range(1, n):
        acc = acc + buf[k]
    o_ref[...] = acc


def scatter_sum(x, axis, cid):
    n = lax.axis_size(axis)
    rows = x.shape[0] // n
    lanes = x.shape[1]
    return pl.pallas_call(
        functools.partial(_scatter_kernel, axis, n),
        out_shape=jax.ShapeDtypeStruct((rows, lanes), jnp.float32),
        in_specs=[pl.BlockSpec(memory_space=pltpu.VMEM)],
        out_specs=pl.BlockSpec(memory_space=pltpu.VMEM),
        scratch_shapes=[
            pltpu.VMEM((n, rows, lanes), jnp.float32),
            pltpu.SemaphoreType.DMA((n,)),
            pltpu.SemaphoreType.DMA((n,)),
        ],
        compiler_params=pltpu.CompilerParams(collective_id=cid, has_side_effects=True),
    )(x.reshape(n, rows, lanes))


_IDS = {("cap", "lse"): 0, ("img", "lse"): 1, ("cap", "sum"): 2, ("img", "sum"): 3}


def gathered_lse(part, axis):
    return combine(part, axis, lax.axis_size(axis), "lse", _IDS[(axis, "lse")])


def gathered_sum(part, axis):
    return combine(part, axis, lax.axis_size(axis), "sum", _IDS[(axis, "sum")])


TM = 1024
TM_PASS = 4096
INV_EPS = 1.0 / SMOOTHING


def _scores_t(img_ref, cap_ref, inv_root):
    return lax.dot_general(
        cap_ref[...], img_ref[...], (((1,), (1,)), ((), ())), preferred_element_type=jnp.float32
    ) * inv_root


def _lane_chunks(x):
    return [x[:, k * 128:(k + 1) * 128] for k in range(x.shape[1] // 128)]


def _row_kernel(mode, inv_root, img_ref, cap_ref, a_ref, b_ref, w_ref, o_ref):
    s = _scores_t(img_ref, cap_ref, inv_root)
    if mode == "lse":
        x = (b_ref[...] + s) * INV_EPS
        top = jnp.max(x, axis=0, keepdims=True)
        o_ref[...] = top + jnp.log(jnp.sum(jnp.exp(x - top), axis=0, keepdims=True))
    else:
        plan = jnp.exp((a_ref[...] + s) * INV_EPS - b_ref[...])
        o_ref[...] = jnp.sum(plan * w_ref[...], axis=0, keepdims=True)


def _specs(n, c, e):
    return [
        pl.BlockSpec((TM_PASS, e), lambda i: (i, 0)),
        pl.BlockSpec((c, e), lambda i: (0, 0)),
        pl.BlockSpec((1, TM_PASS), lambda i: (0, i)),
        pl.BlockSpec((c, 1), lambda i: (0, 0)),
    ]


def row_pass(mode, images, captions, a, b, w):
    n, e = images.shape
    c = captions.shape[0]
    inv_root = 1.0 / math.sqrt(e)
    out = pl.pallas_call(
        functools.partial(_row_kernel, mode, inv_root),
        out_shape=jax.ShapeDtypeStruct((1, n), jnp.float32),
        grid=(n // TM_PASS,),
        in_specs=_specs(n, c, e) + [pl.BlockSpec((c, 1), lambda i: (0, 0))],
        out_specs=pl.BlockSpec((1, TM_PASS), lambda i: (0, i)),
        cost_estimate=pl.CostEstimate(
            flops=2 * n * c * e, transcendentals=n * c, bytes_accessed=n * e * 2 + c * e * 2
        ),
    )(images, captions, a.reshape(1, n), b.reshape(c, 1), w.reshape(c, 1))
    return out.reshape(n)


def _col_kernel(mode, inv_root, img_ref, cap_ref, a_ref, b_ref, w_ref, o_ref, top_ref, tot_ref):
    step = pl.program_id(0)
    s = _scores_t(img_ref, cap_ref, inv_root)
    if mode == "lse":
        chunks = _lane_chunks((a_ref[...] + s) * INV_EPS)

        @pl.when(step == 0)
        def _():
            top_ref[...] = jnp.full(top_ref.shape, -jnp.inf, jnp.float32)
            tot_ref[...] = jnp.zeros(tot_ref.shape, jnp.float32)

        cmax = chunks[0]
        for piece in chunks[1:]:
            cmax = jnp.maximum(cmax, piece)
        old = top_ref[...]
        top = jnp.maximum(old, cmax)
        tot = tot_ref[...] * jnp.exp(old - top)
        for piece in chunks:
            tot = tot + jnp.exp(piece - top)
        tot_ref[...] = tot
        top_ref[...] = top

        @pl.when(step == pl.num_programs(0) - 1)
        def _():
            t = top_ref[...]
            m = jnp.max(t, axis=1, keepdims=True)
            o_ref[...] = m + jnp.log(jnp.sum(tot_ref[...] * jnp.exp(t - m), axis=1, keepdims=True))
    else:
        plan = jnp.exp((b_ref[...] + s) * INV_EPS - a_ref[...])
        chunks = _lane_chunks(plan * w_ref[...])

        @pl.when(step == 0)
        def _():
            tot_ref[...] = jnp.zeros(tot_ref.shape, jnp.float32)

        acc = chunks[0]
        for piece in chunks[1:]:
            acc = acc + piece
        tot_ref[...] += acc

        @pl.when(step == pl.num_programs(0) - 1)
        def _():
            o_ref[...] = jnp.sum(tot_ref[...], axis=1, keepdims=True)


def col_pass(mode, images, captions, a, w, b):
    n, e = images.shape
    c = captions.shape[0]
    inv_root = 1.0 / math.sqrt(e)
    out = pl.pallas_call(
        functools.partial(_col_kernel, mode, inv_root),
        out_shape=jax.ShapeDtypeStruct((c, 1), jnp.float32),
        grid=(n // TM_PASS,),
        in_specs=_specs(n, c, e) + [pl.BlockSpec((1, TM_PASS), lambda i: (0, i))],
        out_specs=pl.BlockSpec((c, 1), lambda i: (0, 0)),
        scratch_shapes=[pltpu.VMEM((c, 128), jnp.float32), pltpu.VMEM((c, 128), jnp.float32)],
        cost_estimate=pl.CostEstimate(
            flops=2 * n * c * e, transcendentals=n * c, bytes_accessed=n * e * 2 + c * e * 2
        ),
    )(images, captions, a.reshape(1, n), b.reshape(c, 1), w.reshape(1, n))
    return out.reshape(c)


def _final_kernel(inv_root, img_ref, cap_ref, rows_ref, cols_ref, ig_ref, cg_ref):
    step = pl.program_id(0)
    s = _scores_t(img_ref, cap_ref, inv_root)
    rows = rows_ref[...]
    cols = cols_ref[...]
    logw_r = rows[6:7, :]
    logw_c = cols[:, 7:8]
    adjoint = jnp.zeros(s.shape, jnp.float32)
    for level in reversed(range(ITERS)):
        f = rows[level:level + 1, :]
        fb = rows[3 + level:4 + level, :]
        g_prev = cols[:, level:level + 1]
        g = cols[:, level + 1:level + 2]
        gb = cols[:, 4 + level:5 + level]
        col_plan = jnp.exp((f + s) * INV_EPS - (logw_c - g * INV_EPS))
        adjoint = adjoint - col_plan * gb
        row_plan = jnp.exp((g_prev + s) * INV_EPS - (logw_r - f * INV_EPS))
        adjoint = adjoint - row_plan * fb
    rounded = adjoint.astype(jnp.bfloat16)
    ig_ref[...] = lax.dot_general(
        rounded, cap_ref[...], (((0,), (0,)), ((), ())), preferred_element_type=jnp.float32
    ) * inv_root

    @pl.when(step == 0)
    def _():
        cg_ref[...] = jnp.zeros(cg_ref.shape, jnp.float32)

    cg_ref[...] += jnp.dot(rounded, img_ref[...], preferred_element_type=jnp.float32) * inv_root


def final_pass(images, captions, rows, cols):
    n, e = images.shape
    c = captions.shape[0]
    inv_root = 1.0 / math.sqrt(e)
    return pl.pallas_call(
        functools.partial(_final_kernel, inv_root),
        out_shape=(
            jax.ShapeDtypeStruct((n, e), jnp.float32),
            jax.ShapeDtypeStruct((c, e), jnp.float32),
        ),
        grid=(n // TM,),
        in_specs=[
            pl.BlockSpec((TM, e), lambda i: (i, 0)),
            pl.BlockSpec((c, e), lambda i: (0, 0)),
            pl.BlockSpec((8, TM), lambda i: (0, i)),
            pl.BlockSpec((c, 8), lambda i: (0, 0)),
        ],
        out_specs=(
            pl.BlockSpec((TM, e), lambda i: (i, 0)),
            pl.BlockSpec((c, e), lambda i: (0, 0)),
        ),
        cost_estimate=pl.CostEstimate(
            flops=6 * n * c * e, transcendentals=6 * n * c, bytes_accessed=n * e * 6 + c * e * 6
        ),
    )(images, captions, rows, cols)


def body(images, captions, image_logw, caption_logw, image_cot, caption_cot):
    n = images.shape[0]
    c = captions.shape[0]
    zeros_r = jnp.zeros((n,), jnp.float32)
    zeros_c = jnp.zeros((c,), jnp.float32)
    col_hist = [zeros_c]
    row_hist = []
    for level in range(ITERS):
        part = row_pass("lse", images, captions, zeros_r, col_hist[-1], zeros_c)
        row_pot = SMOOTHING * image_logw - SMOOTHING * gathered_lse(part, "cap")
        row_hist.append(row_pot)
        part = col_pass("lse", images, captions, row_pot, zeros_r, zeros_c)
        col_hist.append(SMOOTHING * caption_logw - SMOOTHING * gathered_lse(part, "img"))
    col_bar = caption_cot
    row_bars = [None] * ITERS
    col_bars = [None] * ITERS
    for level in reversed(range(ITERS)):
        col_bars[level] = col_bar
        shift_col = caption_logw - col_hist[level + 1] / SMOOTHING
        part = row_pass("wsum", images, captions, row_hist[level], shift_col, col_bar)
        row_bar = -gathered_sum(part, "cap")
        if level == ITERS - 1:
            row_bar = image_cot + row_bar
        row_bars[level] = row_bar
        if level > 0:
            shift_row = image_logw - row_hist[level] / SMOOTHING
            part = col_pass("wsum", images, captions, shift_row, row_bar, col_hist[level])
            col_bar = -gathered_sum(part, "img")
    rows = jnp.stack(row_hist + row_bars + [image_logw, zeros_r], axis=0)
    cols = jnp.stack(col_hist + col_bars + [caption_logw], axis=1)
    ig_part, cg_part = final_pass(images, captions, rows, cols)
    image_grad = lax.psum_scatter(ig_part, "cap", scatter_dimension=0, tiled=True)
    caption_grad = scatter_sum(cg_part, "img", 4)
    return (image_grad, caption_grad)


def solution(mesh):
    in_specs = (P("img", None), P("cap", None), P("img"), P("cap"), P("img"), P("cap"))
    out_specs = (P(("img", "cap"), None), P(("cap", "img"), None))
    return jax.shard_map(body, mesh=mesh, in_specs=in_specs, out_specs=out_specs, check_vma=False)
```

```python
import functools
import math

import jax
import jax.numpy as jnp
from jax import lax
from jax.experimental import pallas as pl
from jax.experimental.pallas import tpu as pltpu

MESH = pl.DeviceIdType.MESH


def _peer(axis, k, n):
    me_img = lax.axis_index("img")
    me_cap = lax.axis_index("cap")
    if axis == "cap":
        return (me_img, lax.rem(me_cap + k, n))
    return (lax.rem(me_img + k, n), me_cap)


def _combine_kernel(axis, n, mode, x_ref, add_ref, o_ref, buf, send_sem, recv_sem):
    barrier = pltpu.get_barrier_semaphore()
    for k in range(1, n):
        pl.semaphore_signal(barrier, inc=1, device_id=_peer(axis, k, n), device_id_type=MESH)
    pl.semaphore_wait(barrier, n - 1)
    copies = []
    for k in range(1, n):
        copy = pltpu.make_async_remote_copy(
            src_ref=x_ref,
            dst_ref=buf.at[k],
            send_sem=send_sem.at[k],
            recv_sem=recv_sem.at[k],
            device_id=_peer(axis, k, n),
            device_id_type=MESH,
        )
        copy.start()
        copies.append(copy)
    for copy in copies:
        copy.wait()
    x = x_ref[...]
    if mode != "lse":
        acc = x
        for k in range(1, n):
            acc = acc + buf[k]
    else:
        top = x
        for k in range(1, n):
            top = jnp.maximum(top, buf[k])
        tot = jnp.exp(x - top)
        for k in range(1, n):
            tot = tot + jnp.exp(buf[k] - top)
        acc = top + jnp.log(tot)
    if mode == "lse":
        o_ref[...] = SMOOTHING * add_ref[...] - SMOOTHING * acc
    elif mode == "sum+":
        o_ref[...] = add_ref[...] + (-acc)
    else:
        o_ref[...] = -acc


def combine(x, axis, n, mode, cid, addend):
    size = x.shape[0]
    rows = size // 128
    x2 = x.reshape(rows, 128)
    out = pl.pallas_call(
        functools.partial(_combine_kernel, axis, n, mode),
        out_shape=jax.ShapeDtypeStruct((rows, 128), jnp.float32),
        in_specs=[pl.BlockSpec(memory_space=pltpu.VMEM)] * 2,
        out_specs=pl.BlockSpec(memory_space=pltpu.VMEM),
        scratch_shapes=[
            pltpu.VMEM((n, rows, 128), jnp.float32),
            pltpu.SemaphoreType.DMA((n,)),
            pltpu.SemaphoreType.DMA((n,)),
        ],
        compiler_params=pltpu.CompilerParams(collective_id=cid, has_side_effects=True),
    )(x2, addend.reshape(rows, 128))
    return out.reshape(size)

from jax.sharding import PartitionSpec as P

ITERS = 3


SMOOTHING = 0.25


def _scatter_kernel(axis, n, x_ref, o_ref, buf, send_sem, recv_sem):
    me = lax.axis_index(axis)
    barrier = pltpu.get_barrier_semaphore()
    for k in range(1, n):
        pl.semaphore_signal(barrier, inc=1, device_id=_peer(axis, k, n), device_id_type=MESH)
    pl.semaphore_wait(barrier, n - 1)
    copies = []
    for k in range(1, n):
        copy = pltpu.make_async_remote_copy(
            src_ref=x_ref.at[lax.rem(me + k, n)],
            dst_ref=buf.at[k],
            send_sem=send_sem.at[k],
            recv_sem=recv_sem.at[k],
            device_id=_peer(axis, k, n),
            device_id_type=MESH,
        )
        copy.start()
        copies.append(copy)
    for copy in copies:
        copy.wait()
    acc = x_ref[me]
    for k in range(1, n):
        acc = acc + buf[k]
    o_ref[...] = acc


def scatter_sum(x, axis, cid):
    n = lax.axis_size(axis)
    rows = x.shape[0] // n
    lanes = x.shape[1]
    return pl.pallas_call(
        functools.partial(_scatter_kernel, axis, n),
        out_shape=jax.ShapeDtypeStruct((rows, lanes), jnp.float32),
        in_specs=[pl.BlockSpec(memory_space=pltpu.VMEM)],
        out_specs=pl.BlockSpec(memory_space=pltpu.VMEM),
        scratch_shapes=[
            pltpu.VMEM((n, rows, lanes), jnp.float32),
            pltpu.SemaphoreType.DMA((n,)),
            pltpu.SemaphoreType.DMA((n,)),
        ],
        compiler_params=pltpu.CompilerParams(collective_id=cid, has_side_effects=True),
    )(x.reshape(n, rows, lanes))


_IDS = {("cap", "lse"): 0, ("img", "lse"): 1, ("cap", "sum"): 2, ("img", "sum"): 3, ("cap", "sum+"): 5}


def potential(part, axis, logw):
    return combine(part, axis, lax.axis_size(axis), "lse", _IDS[(axis, "lse")], logw)


def neg_sum(part, axis, addend=None):
    if addend is None:
        return combine(part, axis, lax.axis_size(axis), "sum", _IDS[(axis, "sum")], part)
    return combine(part, axis, lax.axis_size(axis), "sum+", _IDS[(axis, "sum+")], addend)


TM = 1024
TM_PASS = 2048
INV_EPS = 1.0 / SMOOTHING


def _scores_t(img_ref, cap_ref, inv_root):
    return lax.dot_general(
        cap_ref[...], img_ref[...], (((1,), (1,)), ((), ())), preferred_element_type=jnp.float32
    ) * inv_root


def _lane_chunks(x):
    return [x[:, k * 128:(k + 1) * 128] for k in range(x.shape[1] // 128)]


def _row_kernel(mode, inv_root, img_ref, cap_ref, a_ref, b_ref, w_ref, o_ref):
    s = _scores_t(img_ref, cap_ref, inv_root)
    if mode == "lse":
        x = (b_ref[...] + s) * INV_EPS
        top = jnp.max(x, axis=0, keepdims=True)
        o_ref[...] = top + jnp.log(jnp.sum(jnp.exp(x - top), axis=0, keepdims=True))
    else:
        plan = jnp.exp((a_ref[...] + s) * INV_EPS - b_ref[...])
        o_ref[...] = jnp.sum(plan * w_ref[...], axis=0, keepdims=True)


def _specs(n, c, e):
    return [
        pl.BlockSpec((TM_PASS, e), lambda i: (i, 0)),
        pl.BlockSpec((c, e), lambda i: (0, 0)),
        pl.BlockSpec((1, TM_PASS), lambda i: (0, i)),
        pl.BlockSpec((c, 1), lambda i: (0, 0)),
    ]


def row_pass(mode, images, captions, a, b, w):
    n, e = images.shape
    c = captions.shape[0]
    inv_root = 1.0 / math.sqrt(e)
    out = pl.pallas_call(
        functools.partial(_row_kernel, mode, inv_root),
        out_shape=jax.ShapeDtypeStruct((1, n), jnp.float32),
        grid=(n // TM_PASS,),
        in_specs=_specs(n, c, e) + [pl.BlockSpec((c, 1), lambda i: (0, 0))],
        out_specs=pl.BlockSpec((1, TM_PASS), lambda i: (0, i)),
        cost_estimate=pl.CostEstimate(
            flops=2 * n * c * e, transcendentals=n * c, bytes_accessed=n * e * 2 + c * e * 2
        ),
    )(images, captions, a.reshape(1, n), b.reshape(c, 1), w.reshape(c, 1))
    return out.reshape(n)


def _col_kernel(mode, inv_root, img_ref, cap_ref, a_ref, b_ref, w_ref, o_ref, top_ref, tot_ref):
    step = pl.program_id(0)
    s = _scores_t(img_ref, cap_ref, inv_root)
    if mode == "lse":
        chunks = _lane_chunks((a_ref[...] + s) * INV_EPS)

        @pl.when(step == 0)
        def _():
            top_ref[...] = jnp.full(top_ref.shape, -jnp.inf, jnp.float32)
            tot_ref[...] = jnp.zeros(tot_ref.shape, jnp.float32)

        cmax = chunks[0]
        for piece in chunks[1:]:
            cmax = jnp.maximum(cmax, piece)
        old = top_ref[...]
        top = jnp.maximum(old, cmax)
        tot = tot_ref[...] * jnp.exp(old - top)
        for piece in chunks:
            tot = tot + jnp.exp(piece - top)
        tot_ref[...] = tot
        top_ref[...] = top

        @pl.when(step == pl.num_programs(0) - 1)
        def _():
            t = top_ref[...]
            m = jnp.max(t, axis=1, keepdims=True)
            o_ref[...] = m + jnp.log(jnp.sum(tot_ref[...] * jnp.exp(t - m), axis=1, keepdims=True))
    else:
        plan = jnp.exp((b_ref[...] + s) * INV_EPS - a_ref[...])
        chunks = _lane_chunks(plan * w_ref[...])

        @pl.when(step == 0)
        def _():
            tot_ref[...] = jnp.zeros(tot_ref.shape, jnp.float32)

        acc = chunks[0]
        for piece in chunks[1:]:
            acc = acc + piece
        tot_ref[...] += acc

        @pl.when(step == pl.num_programs(0) - 1)
        def _():
            o_ref[...] = jnp.sum(tot_ref[...], axis=1, keepdims=True)


def col_pass(mode, images, captions, a, w, b):
    n, e = images.shape
    c = captions.shape[0]
    inv_root = 1.0 / math.sqrt(e)
    out = pl.pallas_call(
        functools.partial(_col_kernel, mode, inv_root),
        out_shape=jax.ShapeDtypeStruct((c, 1), jnp.float32),
        grid=(n // TM_PASS,),
        in_specs=_specs(n, c, e) + [pl.BlockSpec((1, TM_PASS), lambda i: (0, i))],
        out_specs=pl.BlockSpec((c, 1), lambda i: (0, 0)),
        scratch_shapes=[pltpu.VMEM((c, 128), jnp.float32), pltpu.VMEM((c, 128), jnp.float32)],
        cost_estimate=pl.CostEstimate(
            flops=2 * n * c * e, transcendentals=n * c, bytes_accessed=n * e * 2 + c * e * 2
        ),
    )(images, captions, a.reshape(1, n), b.reshape(c, 1), w.reshape(1, n))
    return out.reshape(c)


def _final_kernel(inv_root, img_ref, cap_ref, rows_ref, cols_ref, ig_ref, cg_ref):
    step = pl.program_id(0)
    s = _scores_t(img_ref, cap_ref, inv_root)
    rows = rows_ref[...]
    cols = cols_ref[...]
    logw_r = rows[6:7, :]
    logw_c = cols[:, 7:8]
    adjoint = jnp.zeros(s.shape, jnp.float32)
    for level in reversed(range(ITERS)):
        f = rows[level:level + 1, :]
        fb = rows[3 + level:4 + level, :]
        g_prev = cols[:, level:level + 1]
        g = cols[:, level + 1:level + 2]
        gb = cols[:, 4 + level:5 + level]
        col_plan = jnp.exp((f + s) * INV_EPS - (logw_c - g * INV_EPS))
        adjoint = adjoint - col_plan * gb
        row_plan = jnp.exp((g_prev + s) * INV_EPS - (logw_r - f * INV_EPS))
        adjoint = adjoint - row_plan * fb
    rounded = adjoint.astype(jnp.bfloat16)
    ig_ref[...] = lax.dot_general(
        rounded, cap_ref[...], (((0,), (0,)), ((), ())), preferred_element_type=jnp.float32
    ) * inv_root

    @pl.when(step == 0)
    def _():
        cg_ref[...] = jnp.zeros(cg_ref.shape, jnp.float32)

    cg_ref[...] += jnp.dot(rounded, img_ref[...], preferred_element_type=jnp.float32) * inv_root


def final_pass(images, captions, rows, cols):
    n, e = images.shape
    c = captions.shape[0]
    inv_root = 1.0 / math.sqrt(e)
    return pl.pallas_call(
        functools.partial(_final_kernel, inv_root),
        out_shape=(
            jax.ShapeDtypeStruct((n, e), jnp.float32),
            jax.ShapeDtypeStruct((c, e), jnp.float32),
        ),
        grid=(n // TM,),
        in_specs=[
            pl.BlockSpec((TM, e), lambda i: (i, 0)),
            pl.BlockSpec((c, e), lambda i: (0, 0)),
            pl.BlockSpec((8, TM), lambda i: (0, i)),
            pl.BlockSpec((c, 8), lambda i: (0, 0)),
        ],
        out_specs=(
            pl.BlockSpec((TM, e), lambda i: (i, 0)),
            pl.BlockSpec((c, e), lambda i: (0, 0)),
        ),
        cost_estimate=pl.CostEstimate(
            flops=6 * n * c * e, transcendentals=6 * n * c, bytes_accessed=n * e * 6 + c * e * 6
        ),
    )(images, captions, rows, cols)


def body(images, captions, image_logw, caption_logw, image_cot, caption_cot):
    n = images.shape[0]
    c = captions.shape[0]
    zeros_r = jnp.zeros((n,), jnp.float32)
    zeros_c = jnp.zeros((c,), jnp.float32)
    col_hist = [zeros_c]
    row_hist = []
    for level in range(ITERS):
        part = row_pass("lse", images, captions, zeros_r, col_hist[-1], zeros_c)
        row_pot = potential(part, "cap", image_logw)
        row_hist.append(row_pot)
        part = col_pass("lse", images, captions, row_pot, zeros_r, zeros_c)
        col_hist.append(potential(part, "img", caption_logw))
    col_bar = caption_cot
    row_bars = [None] * ITERS
    col_bars = [None] * ITERS
    for level in reversed(range(ITERS)):
        col_bars[level] = col_bar
        shift_col = caption_logw - col_hist[level + 1] / SMOOTHING
        part = row_pass("wsum", images, captions, row_hist[level], shift_col, col_bar)
        row_bar = neg_sum(part, "cap", image_cot if level == ITERS - 1 else None)
        row_bars[level] = row_bar
        if level > 0:
            shift_row = image_logw - row_hist[level] / SMOOTHING
            part = col_pass("wsum", images, captions, shift_row, row_bar, col_hist[level])
            col_bar = neg_sum(part, "img")
    rows = jnp.stack(row_hist + row_bars + [image_logw, zeros_r], axis=0)
    cols = jnp.stack(col_hist + col_bars + [caption_logw], axis=1)
    ig_part, cg_part = final_pass(images, captions, rows, cols)
    image_grad = lax.psum_scatter(ig_part, "cap", scatter_dimension=0, tiled=True)
    caption_grad = scatter_sum(cg_part, "img", 4)
    return (image_grad, caption_grad)


def solution(mesh):
    in_specs = (P("img", None), P("cap", None), P("img"), P("cap"), P("img"), P("cap"))
    out_specs = (P(("img", "cap"), None), P(("cap", "img"), None))
    return jax.shard_map(body, mesh=mesh, in_specs=in_specs, out_specs=out_specs, check_vma=False)
```
